512 devices in a mesh: rows: 16 (over z), cols: 8 (over y, core), layers: 4 (over x).
Axes of the slice: x: 4, y: 4, z: 16, core: 2. Of those that a mesh axis runs over, the one named last changes fastest.
Arguments:
- bottom_known_vector: float32 [768, 128, 256], P(('rows', 'layers')), may hold values from -6 to 6
- bottom_pivot_reciprocal: float32 [768, 128, 128], P(('rows', 'layers'), 'cols'), as said below
- leaf_blocks: float32 [768, 8, 128, 128], P(('rows', 'layers'), 'cols'), may hold values from -0.02734375 to 0.02734375
- leaf_target: int32 [768, 8], P(('rows', 'layers'), 'cols'), may hold values from 0 to 15, as said below
- top_rhs: float32 [16, 128, 256], P('rows'), may hold values from -6 to 6
- top_inv: float32 [16, 128, 128], P('rows'), as said below
- top_sub: float32 [16, 128, 128], P('rows'), may hold values from -0.4375 to 0.4375
Outputs:
- leaf_solution: float32 [768, 128, 256], P(('rows', 'layers'), 'cols')
- top_solution: float32 [16, 128, 256], P('rows')
The draws below stay inside these ranges and needn't reach their ends.
Inputs may be any that keep to these rules, and one draw needn't show every extreme that they name: `leaf_target`: each leaf names 8 different top supernodes. `bottom_pivot_reciprocal`: each block is its diagonal times a factor of 0.7 to 1.3 plus a full-rank off-diagonal part. `top_inv`: each block is its diagonal times a factor of 0.7 to 1.3 plus a full-rank off-diagonal part.
All inputs are finite; a program needn't handle non-finite values.
Results may differ from the reference program's by a relative error of at most 0.00028.
Values sent between devices are 32-bit elements; how exact they have to be, the bound alone decides.
No kernel may reach another device: no remote copies, remote signals or barrier semaphores. Data moves between devices by JAX's collectives and lax.ppermute only.
A program may use at most 64 MiB of HBM per device.

```python
import math
import jax
import jax.numpy as jnp
from jax import lax

B = 128
R = 256
LDEV = 12
NT = 16
P_SIZE = 8
LEAVES = 768
N_COLS = 8
N_LAYERS = 4


def draw_bottom_pivot_reciprocal(key, part):
    key_diag, key_off = jax.random.split(jax.random.fold_in(key, 11))
    diag_scale = jax.random.uniform(key_diag, (LEAVES, B, 1), jnp.float32, 0.7, 1.3)
    identity = (jnp.arange(B)[:, None] == jnp.arange(B)[None, :]).astype(jnp.float32)
    off_diag = jax.random.normal(key_off, (LEAVES, B, B), jnp.float32) * (0.4 / math.sqrt(B))
    return identity * diag_scale + off_diag


def draw_top_inv(key, part):
    key_diag, key_off = jax.random.split(jax.random.fold_in(key, 23))
    diag_scale = jax.random.uniform(key_diag, (NT, B, 1), jnp.float32, 0.7, 1.3)
    identity = (jnp.arange(B)[:, None] == jnp.arange(B)[None, :]).astype(jnp.float32)
    off_diag = jax.random.normal(key_off, (NT, B, B), jnp.float32) * (0.4 / math.sqrt(B))
    return identity * diag_scale + off_diag


def pick_row(random_seed_entry):
    return jax.random.permutation(random_seed_entry, NT)[:P_SIZE].astype(jnp.int32)


def draw_leaf_target(key, part):
    row_keys = jax.random.split(jax.random.fold_in(key, 37), LEAVES)
    return jax.vmap(pick_row)(row_keys)


def shard_levels(own_key, dims, cuts, least, largest):
    gain = 1.0
    for dim, shards_of in cuts:
        draws = jax.random.uniform(jax.random.fold_in(jax.random.fold_in(own_key, 6), dim), (shards_of,), jnp.float32, least / len(cuts), largest / len(cuts))
        gain = gain * jnp.repeat(jnp.exp(draws), dims[dim] // shards_of).reshape((-1,) + (1,) * (len(dims) - 1 - dim))
    return gain


def gaussian(stream_key, shape, spread, bound, cuts=(), kind=jnp.bfloat16):
    values = jax.random.normal(stream_key, shape, jnp.float32) * spread
    if len(cuts) > 0:
        values = shard_levels(stream_key, shape, cuts, -0.22, 0.18) * values
    return jnp.clip(values, min=-bound, max=bound).astype(kind)


def setup_inputs(seed: int = 0) -> dict:
    seeds = jax.random.split(jax.random.key(seed), 8)
    return {
        "bottom_known_vector": gaussian(seeds[0], (LEAVES, B, R), 1.0, 6.0, ((0, 64),), jnp.float32),
        "bottom_pivot_reciprocal": draw_bottom_pivot_reciprocal(jax.random.fold_in(seeds[7], 71), 0),
        "leaf_blocks": gaussian(seeds[2], (LEAVES, P_SIZE, B, B), (B * LDEV * N_LAYERS * N_COLS) ** -0.5, 0.02734375, ((0, 64), (1, 8)), jnp.float32),
        "leaf_target": draw_leaf_target(jax.random.fold_in(seeds[7], 71), 0),
        "top_rhs": gaussian(seeds[4], (NT, B, R), 1.0, 6.0, ((0, 16),), jnp.float32),
        "top_inv": draw_top_inv(jax.random.fold_in(seeds[7], 71), 0),
        "top_sub": gaussian(seeds[6], (NT, B, B), (B * 3 // 2) ** -0.5, 0.4375, ((0, 16),), jnp.float32),
    }


def reference(bottom_known_vector, bottom_pivot_reciprocal, leaf_blocks, leaf_target, top_rhs, top_inv, top_sub):
    exact_arithmetic_mode = lax.Precision.HIGHEST
    leaf_forward = jnp.einsum('jab,jbr->jar', bottom_pivot_reciprocal, bottom_known_vector, precision=exact_arithmetic_mode)

    def propagate_update(summed, leaf_item):
        blocks, solved, targets = leaf_item
        contrib = jnp.einsum('pab,br->par', blocks, solved, precision=exact_arithmetic_mode)
        return summed.at[targets].add(contrib), None

    carried, unused = lax.scan(propagate_update, jnp.zeros((NT, B, R), jnp.float32), (leaf_blocks, leaf_forward, leaf_target))

    def forward_step(previous, top_item):
        diag_inv, rhs_part, coupling = top_item
        solved = jnp.dot(diag_inv, rhs_part - jnp.dot(coupling, previous, precision=exact_arithmetic_mode), precision=exact_arithmetic_mode)
        return solved, solved

    start_zero = jnp.zeros((B, R), jnp.float32)
    unused_last, top_forward = lax.scan(forward_step, start_zero, (top_inv, top_rhs - carried, top_sub))
    coupling_next = jnp.concatenate([top_sub[1:], jnp.zeros((1, B, B), jnp.float32)], axis=0)

    def backward_step(following, top_item):
        diag_inv, forward_portion, coupling = top_item
        solved = jnp.dot(diag_inv.T, forward_portion - jnp.dot(coupling.T, following, precision=exact_arithmetic_mode), precision=exact_arithmetic_mode)
        return solved, solved

    unused_first, top_solution = lax.scan(backward_step, start_zero, (top_inv, top_forward, coupling_next), reverse=True)

    def leaf_step(leaf_item):
        diag_inv, blocks, solved, targets = leaf_item
        picked = top_solution[targets]
        back_sum = jnp.einsum('pab,par->br', blocks, picked, precision=exact_arithmetic_mode)
        return jnp.dot(diag_inv.T, solved - back_sum, precision=exact_arithmetic_mode)

    leaf_solution = lax.map(leaf_step, (bottom_pivot_reciprocal, leaf_blocks, leaf_forward, leaf_target))
    return leaf_solution, top_solution
```

```python
import jax
import jax.numpy as jnp
from jax import lax
from jax.experimental import pallas as pl
from jax.experimental.pallas import tpu as pltpu
from jax.sharding import Mesh, PartitionSpec as P

F32 = jnp.float32
BF16 = jnp.bfloat16
ROWS = ("rhi", "rlo")
EXACT = lax.Precision.HIGHEST


def dot(a, b, ca=1, cb=0):
    return lax.dot_general(
        a, b, (((ca,), (cb,)), ((), ())), precision=EXACT, preferred_element_type=F32
    )


def split(x):
    high = x.astype(BF16)
    low = (x - high.astype(F32)).astype(BF16)
    return high, low


def split_dot(x, pair):
    n = x.shape[0]
    m = pair.shape[1] // 2
    rows = jnp.concatenate(split(x), axis=0)
    r = lax.dot_general(rows, pair, (((1,), (0,)), ((), ())), preferred_element_type=F32)
    return (r[:n, :m] + (r[n:, :m] + r[:n, m:])) + r[n:, m:]


def whole(shape):
    return pl.BlockSpec(shape, lambda *_: (0,) * len(shape))


def leaf_forward_kernel(leaves, targets_ref, col_ref, inv_ref, blocks_ref, known_ref, sums_ref, own_ref):
    leaf = pl.program_id(0)

    @pl.when(leaf == 0)
    def _():
        sums_ref[...] = jnp.zeros_like(sums_ref)

    forward = dot(known_ref[0].T, inv_ref[0], 1, 1)
    update = dot(forward, blocks_ref[0], 1, 1)
    t = targets_ref[leaf]
    for q in range(sums_ref.shape[0]):
        sums_ref[q, t] += update[8 * q : 8 * q + 8]
    own = own_ref.shape[1]
    parts = forward.shape[0] // own
    col = col_ref[0]
    picked = forward[:own]
    for c in range(1, parts):
        picked = jnp.where(col == c, forward[c * own : (c + 1) * own], picked)
    own_ref[0] = picked


def leaf_forward(targets, col, inv, blocks, known, tops, n_cols):
    leaves, b, r = known.shape
    return pl.pallas_call(
        lambda *refs: leaf_forward_kernel(leaves, *refs),
        grid_spec=pltpu.PrefetchScalarGridSpec(
            num_scalar_prefetch=2,
            grid=(leaves,),
            in_specs=[
                pl.BlockSpec((1, b, b), lambda i, *_: (i, 0, 0)),
                pl.BlockSpec((1, b, b), lambda i, *_: (i, 0, 0)),
                pl.BlockSpec((1, b, r), lambda i, *_: (i, 0, 0)),
            ],
            out_specs=[
                whole((r // 8, tops, 8, b)),
                pl.BlockSpec((1, r // n_cols, b), lambda i, *_: (i, 0, 0)),
            ],
        ),
        out_shape=[
            jax.ShapeDtypeStruct((r // 8, tops, 8, b), F32),
            jax.ShapeDtypeStruct((leaves, r // n_cols, b), F32),
        ],
        name="leaf_forward",
    )(targets, col, inv, blocks, known)


def top_maps_kernel(inv_ref, sub_ref, next_ref, fwd_ref, bwd_ref, inv_t_ref, inv_pair_ref):
    def store(ref, x):
        high, low = split(x)
        m = x.shape[1]
        ref[0, :, :m] = high
        ref[0, :, m:] = low

    a = inv_ref[0]
    store(fwd_ref, -dot(a, sub_ref[0]).T)
    store(bwd_ref, -dot(next_ref[0], a))
    store(inv_t_ref, a.T)
    store(inv_pair_ref, a)


def top_maps(both):
    tops, _, b, _ = both.shape
    pair = jax.ShapeDtypeStruct((tops, b, 2 * b), BF16)
    out = pl.BlockSpec((1, b, 2 * b), lambda i: (i, 0, 0))
    return pl.pallas_call(
        top_maps_kernel,
        grid=(tops,),
        in_specs=[
            pl.BlockSpec((1, None, b, b), lambda i: (i, 0, 0, 0)),
            pl.BlockSpec((1, None, b, b), lambda i: (i, 1, 0, 0)),
            pl.BlockSpec((1, None, b, b), lambda i: (jnp.minimum(i + 1, tops - 1), 1, 0, 0)),
        ],
        out_specs=[out] * 4,
        out_shape=[pair] * 4,
        name="top_maps",
    )(both, both, both)


def top_chain_kernel(rhs_ref, fwd_ref, bwd_ref, inv_t_ref, inv_ref, out_ref):
    tops = rhs_ref.shape[0]
    scaled = []
    current = split_dot(rhs_ref[0], inv_t_ref[0])
    scaled.append(split_dot(current, inv_ref[0]))
    for t in range(1, tops):
        current = split_dot(rhs_ref[t], inv_t_ref[t]) + split_dot(current, fwd_ref[t])
        scaled.append(split_dot(current, inv_ref[t]))
    current = scaled[tops - 1]
    out_ref[tops - 1] = current
    for t in range(tops - 2, -1, -1):
        current = scaled[t] + split_dot(current, bwd_ref[t])
        out_ref[t] = current


def top_chain(rhs, maps):
    return pl.pallas_call(
        top_chain_kernel,
        out_shape=jax.ShapeDtypeStruct(rhs.shape, F32),
        name="top_chain",
    )(rhs, *maps)


def leaf_backward_kernel(targets_ref, tops_ref, blocks_ref, own_ref, inv_ref, out_ref, stage):
    leaf = pl.program_id(0)
    n_cols = blocks_ref.shape[0]
    own = own_ref.shape[1]
    b = own_ref.shape[2]
    left = own_ref[0]
    for p in range(n_cols):
        t = targets_ref[p, leaf]
        left = left - dot(tops_ref[:, t].reshape(own, b), blocks_ref[p, 0])
    group = b // own
    place = leaf % group
    stage[pl.ds(pl.multiple_of(place * own, own), own), :] = dot(left, inv_ref[0])

    @pl.when(place == group - 1)
    def _():
        turned = stage[...].T
        rows = b // n_cols
        for c in range(n_cols):
            out_ref[c, 0] = turned[c * rows : (c + 1) * rows]


def leaf_backward(targets, tops, blocks, own, inv):
    n_cols, leaves, b, _ = blocks.shape
    mine = own.shape[1]
    group = b // mine
    rows = b // n_cols
    return pl.pallas_call(
        leaf_backward_kernel,
        grid_spec=pltpu.PrefetchScalarGridSpec(
            num_scalar_prefetch=1,
            grid=(leaves,),
            in_specs=[
                pl.BlockSpec(tops.shape, lambda i, *_: (0, 0, 0, 0)),
                pl.BlockSpec((n_cols, 1, b, b), lambda i, *_: (0, i, 0, 0)),
                pl.BlockSpec((1, mine, b), lambda i, *_: (i, 0, 0)),
                pl.BlockSpec((1, b, b), lambda i, *_: (i, 0, 0)),
            ],
            out_specs=pl.BlockSpec((n_cols, 1, rows, b), lambda i, *_: (0, i // group, 0, 0)),
            scratch_shapes=[pltpu.VMEM((b, b), F32)],
        ),
        out_shape=jax.ShapeDtypeStruct((n_cols, leaves // group, rows, b), F32),
        name="leaf_backward",
    )(targets, tops, blocks, own, inv)


def arrange_kernel(got_ref, out_ref):
    n_cols, groups, _, lanes = got_ref.shape
    own = out_ref.shape[2] // n_cols
    group = lanes // own
    for g in range(groups):
        for i in range(group):
            for h in range(n_cols // group):
                out_ref[g * group + i, :, h * lanes : (h + 1) * lanes] = jnp.concatenate(
                    [got_ref[h * group + q, g, :, i * own : (i + 1) * own] for q in range(group)],
                    axis=1,
                )


def arrange(got, leaves, r):
    return pl.pallas_call(
        arrange_kernel,
        out_shape=jax.ShapeDtypeStruct((leaves, got.shape[2], r), F32),
        name="arrange",
    )(got)


def on_device(known, pivot, leaf_blocks, leaf_target, top_rhs, top_inv, top_sub):
    leaves, b, r = known.shape
    n_cols = lax.axis_size("cols")
    n_layers = lax.axis_size("layers")
    tops = lax.axis_size(ROWS)
    col = lax.axis_index("cols")
    row = lax.axis_index(ROWS)
    part = col * n_layers + lax.axis_index("layers")
    blocks = leaf_blocks[:, 0]
    slab = pivot.shape[1]

    both = lax.all_gather(jnp.stack([top_inv[0], top_sub[0]]), ROWS, axis=0, tiled=False)
    all_blocks = lax.all_gather(blocks, "cols", axis=0, tiled=False)

    named = jnp.zeros((1, slab, b), F32).at[0, 0, :leaves].set(leaf_target[:, 0].astype(F32))
    gathered = lax.all_gather(jnp.concatenate([pivot, named]), "cols", axis=1, tiled=True)
    all_targets = gathered[leaves].reshape(n_cols, slab, b)[:, 0, :leaves].astype(jnp.int32)

    sums, own = leaf_forward(
        leaf_target[:, 0], col[None], gathered, blocks, known, tops, n_cols
    )
    arrived = lax.all_to_all(sums, ("cols", "layers"), 0, 0, tiled=True)
    rhs_t = lax.dynamic_slice_in_dim(top_rhs[0], part * 8, 8, 1).T
    mine = (jnp.arange(tops) == row)[:, None, None]
    partial = jnp.where(mine, rhs_t[None], 0.0) - arrived.sum(0)

    quarter = lax.all_to_all(partial, "rlo", 0, 0, tiled=True)
    quarter = quarter.reshape((lax.axis_size("rlo"), -1) + quarter.shape[1:]).sum(0)
    quarter = lax.all_gather(quarter, "rhi", axis=0, tiled=False).sum(0)
    rhs = lax.all_gather(quarter, "rlo", axis=0, tiled=True)

    solved = top_chain(rhs, top_maps(both))
    own_tops = lax.all_gather(solved, "layers", axis=0, tiled=False)

    top_cols = lax.dynamic_index_in_dim(own_tops, row, 1, keepdims=False).reshape(1, -1, b)
    top_cols = jnp.broadcast_to(top_cols, (n_cols,) + top_cols.shape[1:])
    top_all = lax.all_to_all(top_cols, "cols", 0, 0, tiled=True)
    top_part = top_all.reshape(r, b).T[None]

    turned = leaf_backward(all_targets, own_tops, all_blocks, own, gathered)
    got = lax.all_to_all(turned, "cols", 0, 0, tiled=True)
    return arrange(got, leaves, r), top_part


def solution(mesh):
    rows = mesh.shape["rows"]
    low = 4 if rows % 4 == 0 else 1
    fine = Mesh(
        mesh.devices.reshape(rows // low, low, mesh.shape["cols"], mesh.shape["layers"]),
        ROWS + ("cols", "layers"),
    )
    held = ROWS + ("layers",)
    in_specs = (
        P(held, None, None),
        P(held, "cols", None),
        P(held, "cols", None, None),
        P(held, "cols"),
        P(ROWS, None, None),
        P(ROWS, None, None),
        P(ROWS, None, None),
    )
    out_specs = (P(held, "cols", None), P(ROWS, None, None))
    return jax.shard_map(
        on_device, mesh=fine, in_specs=in_specs, out_specs=out_specs, check_vma=False
    )
```

```python
import jax
import jax.numpy as jnp
from jax import lax
from jax.experimental import pallas as pl
from jax.experimental.pallas import tpu as pltpu
from jax.sharding import Mesh, PartitionSpec as P

F32 = jnp.float32
BF16 = jnp.bfloat16
ROWS = ("rhi", "rlo")
COLS = ("y", "core")


def dot(a, b, cb=0):
    return lax.dot_general(a, b, (((1,), (cb,)), ((), ())), preferred_element_type=F32)


def split(x):
    high = x.astype(BF16)
    low = (x - high.astype(F32)).astype(BF16)
    return high, low


def dot3(a, b, cb=0):
    ah, al = split(a)
    bh, bl = split(b)
    both = dot(
        jnp.concatenate([ah, al], axis=1), jnp.concatenate([bh, bh], axis=cb), cb
    )
    return both + dot(ah, bl, cb)


def row_dot(x, matrix, cb=0):
    n = x.shape[0]
    m = matrix.shape[1 - cb]
    rows = jnp.concatenate(split(x), axis=0)
    r = dot(rows, jnp.concatenate(split(matrix), axis=1 - cb), cb)
    return (r[:n, :m] + (r[n:, :m] + r[:n, m:])) + r[n:, m:]


def whole(shape):
    return pl.BlockSpec(shape, lambda *_: (0,) * len(shape))


def leaf_forward_kernel(place_ref, targets_ref, inv_ref, mine_ref, pair_ref, known_ref, sums_ref, own_ref, stage):
    leaf = pl.program_id(0)

    @pl.when(leaf == 0)
    def _():
        sums_ref[...] = jnp.zeros_like(sums_ref)

    b = inv_ref.shape[1]
    forward = dot3(known_ref[0].T, inv_ref[0], 1)
    update = dot3(forward, jnp.concatenate([mine_ref[0], pair_ref[0]], axis=0), 1)
    for k in range(2):
        t = targets_ref[k, leaf]
        for q in range(sums_ref.shape[0]):
            sums_ref[q, t] += update[8 * q : 8 * q + 8, k * b : (k + 1) * b]
    own = own_ref.shape[1]
    stage[...] = forward
    own_ref[0] = stage[pl.ds(pl.multiple_of(place_ref[1] * own, own), own), :]


def leaf_forward(place, targets, inv, mine, pair, known, tops, n_cols):
    leaves, b, r = known.shape
    half = r // 2
    own = r // n_cols
    block = pl.BlockSpec((1, b, b), lambda i, *_: (i, 0, 0))
    return pl.pallas_call(
        leaf_forward_kernel,
        grid_spec=pltpu.PrefetchScalarGridSpec(
            num_scalar_prefetch=2,
            grid=(leaves,),
            in_specs=[
                block,
                block,
                block,
                pl.BlockSpec((1, b, half), lambda i, place, _: (i, 0, place[0])),
            ],
            out_specs=[
                whole((half // 8, tops, 8, b)),
                pl.BlockSpec((1, own, b), lambda i, *_: (i, 0, 0)),
            ],
            scratch_shapes=[pltpu.VMEM((half, b), F32)],
        ),
        out_shape=[
            jax.ShapeDtypeStruct((half // 8, tops, 8, b), F32),
            jax.ShapeDtypeStruct((leaves, own, b), F32),
        ],
        name="leaf_forward",
    )(place, targets, inv, mine, pair, known)


def top_map_kernel(inv_ref, sub_ref, out_ref):
    out_ref[0] = inv_ref[0]
    out_ref[1] = -lax.dot_general(
        inv_ref[0],
        sub_ref[0],
        (((1,), (0,)), ((), ())),
        precision=lax.Precision.HIGHEST,
        preferred_element_type=F32,
    )


def top_map(inv, sub):
    return pl.pallas_call(
        top_map_kernel,
        out_shape=jax.ShapeDtypeStruct((2,) + inv.shape[1:], F32),
        name="top_map",
    )(inv, sub)


def top_chain_kernel(rhs_ref, maps_ref, out_ref):
    tops = rhs_ref.shape[0]
    solved = []
    current = row_dot(rhs_ref[0], maps_ref[0, 0], 1)
    solved.append(current)
    for t in range(1, tops):
        current = row_dot(rhs_ref[t], maps_ref[t, 0], 1) + row_dot(current, maps_ref[t, 1], 1)
        solved.append(current)
    rest = solved[tops - 1]
    out_ref[tops - 1] = row_dot(rest, maps_ref[tops - 1, 0])
    for t in range(tops - 2, -1, -1):
        rest = solved[t] + row_dot(rest, maps_ref[t + 1, 1])
        out_ref[t] = row_dot(rest, maps_ref[t, 0])


def top_chain(rhs, maps):
    return pl.pallas_call(
        top_chain_kernel,
        out_shape=jax.ShapeDtypeStruct(rhs.shape, F32),
        name="top_chain",
    )(rhs, maps)


def leaf_backward_kernel(targets_ref, tops_ref, *refs):
    *block_refs, own_ref, inv_ref, out_ref, stage, parts = refs
    leaf = pl.program_id(0)
    n_cols = len(block_refs)
    own = own_ref.shape[1]
    b = own_ref.shape[2]

    @pl.when(leaf == 0)
    def _():
        for t in range(parts.shape[0]):
            high, low = split(tops_ref[:, t].reshape(own, b))
            parts[t, :own] = high
            parts[t, own:] = low

    both = jnp.concatenate([parts[targets_ref[p, leaf]] for p in range(n_cols)], axis=1)
    high, low = split(jnp.concatenate([ref[0] for ref in block_refs], axis=0))
    r = dot(both, high)
    left = own_ref[0] - ((r[:own] + r[own:]) + dot(both[:own], low))
    group = b // own
    place = leaf % group
    stage[pl.ds(pl.multiple_of(place * own, own), own), :] = dot3(left, inv_ref[0])

    @pl.when(place == group - 1)
    def _():
        turned = stage[...].T
        rows = b // n_cols
        for c in range(n_cols):
            out_ref[c, 0] = turned[c * rows : (c + 1) * rows]


def leaf_backward(targets, tops, blocks, own, inv):
    n_cols = len(blocks)
    leaves, b, _ = blocks[0].shape
    mine = own.shape[1]
    group = b // mine
    rows = b // n_cols
    block = pl.BlockSpec((1, b, b), lambda i, *_: (i, 0, 0))
    return pl.pallas_call(
        leaf_backward_kernel,
        grid_spec=pltpu.PrefetchScalarGridSpec(
            num_scalar_prefetch=1,
            grid=(leaves,),
            in_specs=[pl.BlockSpec(tops.shape, lambda i, *_: (0, 0, 0, 0))]
            + [block] * n_cols
            + [pl.BlockSpec((1, mine, b), lambda i, *_: (i, 0, 0)), block],
            out_specs=pl.BlockSpec((n_cols, 1, rows, b), lambda i, *_: (0, i // group, 0, 0)),
            scratch_shapes=[
                pltpu.VMEM((b, b), F32),
                pltpu.VMEM((tops.shape[1], 2 * mine, b), BF16),
            ],
        ),
        out_shape=jax.ShapeDtypeStruct((n_cols, leaves // group, rows, b), F32),
        name="leaf_backward",
    )(targets, tops, *blocks, own, inv)


def arrange_kernel(got_ref, out_ref):
    n_cols, groups, _, lanes = got_ref.shape
    own = out_ref.shape[2] // n_cols
    group = lanes // own
    for g in range(groups):
        for i in range(group):
            for h in range(n_cols // group):
                out_ref[g * group + i, :, h * lanes : (h + 1) * lanes] = jnp.concatenate(
                    [got_ref[2 * q + h, g, :, i * own : (i + 1) * own] for q in range(group)],
                    axis=1,
                )


def arrange(got, leaves, r):
    return pl.pallas_call(
        arrange_kernel,
        out_shape=jax.ShapeDtypeStruct((leaves, got.shape[2], r), F32),
        name="arrange",
    )(got)


def spread(x, axis):
    return lax.all_to_all(jnp.broadcast_to(x, (lax.axis_size(axis),) + x.shape), axis, 0, 0, tiled=True)


def from_core(x):
    return lax.ppermute(x, "core", [(0, 1), (1, 0)])


def from_y(x, step):
    n = lax.axis_size("y")
    return lax.ppermute(x, "y", [(i, (i - step) % n) for i in range(n)])


def on_device(known, pivot, leaf_blocks, leaf_target, top_rhs, top_inv, top_sub):
    leaves, b, r = known.shape
    n_y = lax.axis_size("y")
    n_cols = 2 * n_y
    n_layers = lax.axis_size("layers")
    tops = lax.axis_size(ROWS)
    y = lax.axis_index("y")
    core = lax.axis_index("core")
    row = lax.axis_index(ROWS)
    blocks = leaf_blocks[:, 0]
    slab = pivot.shape[1]
    own = r // n_cols

    maps = lax.all_gather(top_map(top_inv, top_sub), ROWS, axis=0, tiled=False)

    paired = from_core(blocks)
    named = jnp.zeros((1, slab, b), F32).at[0, 0, :leaves].set(leaf_target[:, 0].astype(F32))
    inv = lax.all_gather(jnp.concatenate([pivot, named]), COLS, axis=1, tiled=True)
    targets = inv[leaves].reshape(n_y, 2, slab, b)[:, :, 0, :leaves].astype(jnp.int32)
    targets = jnp.roll(targets, -y, axis=0)
    targets = jnp.where(core == 0, targets, targets[:, ::-1]).reshape(n_cols, leaves)

    sums, own_forward = leaf_forward(
        jnp.stack([core, y]), targets, inv, blocks, paired, known, tops, n_cols
    )
    arrived = lax.all_to_all(sums, ("y", "layers"), 0, 0, tiled=True)
    start = core * (r // 2) + y * own + lax.axis_index("layers") * 8
    rhs_t = lax.dynamic_slice_in_dim(top_rhs[0], start, 8, 1).T
    mine = (jnp.arange(tops) == row)[:, None, None]
    partial = jnp.where(mine, rhs_t[None], 0.0) - arrived.sum(0)

    held, partial = lax.optimization_barrier((blocks, partial))
    far = [from_y(held, step) for step in range(1, n_y)]

    quarter = lax.all_to_all(partial, "rlo", 0, 0, tiled=True)
    quarter = quarter.reshape((lax.axis_size("rlo"), -1) + quarter.shape[1:]).sum(0)
    quarter = spread(quarter, "rhi").reshape((-1,) + quarter.shape).sum(0)
    rhs = spread(quarter, "rlo").reshape(tops, 8, b)

    solved = top_chain(rhs, maps)
    solved, far = lax.optimization_barrier((solved, far))
    all_blocks = [blocks, paired]
    for block in far:
        all_blocks += [block, from_core(block)]
    own_tops = spread(solved, "layers").reshape(n_layers, tops, 8, b)

    top_cols = lax.dynamic_index_in_dim(own_tops, row, 1, keepdims=False).reshape(own, b)
    top_all = spread(top_cols, COLS).reshape(n_y, 2, own, b)
    top_part = top_all.transpose(1, 0, 2, 3).reshape(r, b).T[None]

    turned = leaf_backward(targets, own_tops, all_blocks, own_forward, inv)
    got = lax.all_to_all(turned, COLS, 0, 0, tiled=True)
    return arrange(got, leaves, r), top_part


def solution(mesh):
    rows = mesh.shape["rows"]
    low = 4
    fine = Mesh(
        mesh.devices.reshape(
            rows // low, low, mesh.shape["cols"] // 2, 2, mesh.shape["layers"]
        ),
        ROWS + COLS + ("layers",),
    )
    held = ROWS + ("layers",)
    in_specs = (
        P(held, None, None),
        P(held, COLS, None),
        P(held, COLS, None, None),
        P(held, COLS),
        P(ROWS, None, None),
        P(ROWS, None, None),
        P(ROWS, None, None),
    )
    out_specs = (P(held, COLS, None), P(ROWS, None, None))
    return jax.shard_map(
        on_device, mesh=fine, in_specs=in_specs, out_specs=out_specs, check_vma=False
    )
```

```python
import jax
import jax.numpy as jnp
from jax import lax
from jax.experimental import pallas as pl
from jax.experimental.pallas import tpu as pltpu
from jax.sharding import Mesh, PartitionSpec as P

F32 = jnp.float32
BF16 = jnp.bfloat16
ROWS = ("rhi", "rlo")
COLS = ("y", "core")
STEP = 4


def dot(a, b, cb=0):
    return lax.dot_general(a, b, (((1,), (cb,)), ((), ())), preferred_element_type=F32)


def split(x):
    high = x.astype(BF16)
    low = (x - high.astype(F32)).astype(BF16)
    return high, low


def dot3(a, b, cb=0):
    ah, al = split(a)
    bh, bl = split(b)
    both = dot(
        jnp.concatenate([ah, al], axis=1), jnp.concatenate([bh, bh], axis=cb), cb
    )
    return both + dot(ah, bl, cb)


def row_dot(x, matrix, cb=0):
    n = x.shape[0]
    m = matrix.shape[1 - cb]
    rows = jnp.concatenate(split(x), axis=0)
    r = dot(rows, jnp.concatenate(split(matrix), axis=1 - cb), cb)
    return (r[:n, :m] + (r[n:, :m] + r[:n, m:])) + r[n:, m:]


def whole(shape):
    return pl.BlockSpec(shape, lambda *_: (0,) * len(shape))


def leaf_forward_kernel(place_ref, targets_ref, inv_ref, mine_ref, pair_ref, known_ref, sums_ref, own_ref, stage):
    step = pl.program_id(0)
    count, b = mine_ref.shape[:2]
    own = own_ref.shape[1]

    @pl.when(step == 0)
    def _():
        sums_ref[...] = jnp.zeros_like(sums_ref)

    for i in range(count):
        inv = inv_ref[:, i].reshape(b, b)
        forward = dot3(known_ref[i].T, inv, 1)
        update = dot3(forward, jnp.concatenate([mine_ref[i], pair_ref[i]], axis=0), 1)
        for k in range(2):
            t = targets_ref[k, step * count + i]
            for q in range(sums_ref.shape[0]):
                sums_ref[q, t] += update[8 * q : 8 * q + 8, k * b : (k + 1) * b]
        stage[i] = forward
        own_ref[i] = stage[i, pl.ds(pl.multiple_of(place_ref[1] * own, own), own), :]


def leaf_forward(place, targets, inv, mine, pair, known, tops):
    leaves, b, r = known.shape
    n_cols, _, slab, _ = inv.shape
    half = r // 2
    own = r // n_cols
    block = pl.BlockSpec((STEP, b, b), lambda i, *_: (i, 0, 0))
    return pl.pallas_call(
        leaf_forward_kernel,
        grid_spec=pltpu.PrefetchScalarGridSpec(
            num_scalar_prefetch=2,
            grid=(leaves // STEP,),
            in_specs=[
                pl.BlockSpec((n_cols, STEP, slab, b), lambda i, *_: (0, i, 0, 0)),
                block,
                block,
                pl.BlockSpec((STEP, b, half), lambda i, place, _: (i, 0, place[0])),
            ],
            out_specs=[
                whole((half // 8, tops, 8, b)),
                pl.BlockSpec((STEP, own, b), lambda i, *_: (i, 0, 0)),
            ],
            scratch_shapes=[pltpu.VMEM((STEP, half, b), F32)],
        ),
        out_shape=[
            jax.ShapeDtypeStruct((half // 8, tops, 8, b), F32),
            jax.ShapeDtypeStruct((leaves, own, b), F32),
        ],
        name="leaf_forward",
    )(place, targets, inv, mine, pair, known)


def top_map_kernel(inv_ref, sub_ref, out_ref):
    out_ref[0] = inv_ref[0]
    out_ref[1] = -lax.dot_general(
        inv_ref[0],
        sub_ref[0],
        (((1,), (0,)), ((), ())),
        precision=lax.Precision.HIGHEST,
        preferred_element_type=F32,
    )


def top_map(inv, sub):
    return pl.pallas_call(
        top_map_kernel,
        out_shape=jax.ShapeDtypeStruct((2,) + inv.shape[1:], F32),
        name="top_map",
    )(inv, sub)


def top_chain_kernel(rhs_ref, maps_ref, out_ref):
    low, layers, high, n, b = rhs_ref.shape
    tops = low * high

    def rhs(t):
        return rhs_ref[t // high, :, t % high].reshape(layers * n, b)

    def maps(t, kind):
        return maps_ref[t % low, t // low, kind]

    solved = []
    current = row_dot(rhs(0), maps(0, 0), 1)
    solved.append(current)
    for t in range(1, tops):
        current = row_dot(rhs(t), maps(t, 0), 1) + row_dot(current, maps(t, 1), 1)
        solved.append(current)
    rest = solved[tops - 1]
    out_ref[tops - 1] = row_dot(rest, maps(tops - 1, 0))
    for t in range(tops - 2, -1, -1):
        rest = solved[t] + row_dot(rest, maps(t + 1, 1))
        out_ref[t] = row_dot(rest, maps(t, 0))


def top_chain(rhs, maps):
    low, layers, high, n, b = rhs.shape
    return pl.pallas_call(
        top_chain_kernel,
        out_shape=jax.ShapeDtypeStruct((low * high, layers * n, b), F32),
        name="top_chain",
    )(rhs, maps)


def leaf_backward_kernel(row_ref, targets_ref, tops_ref, blocks_ref, own_ref, inv_ref, out_ref, parts):
    step = pl.program_id(0)
    n_cols, count, b, _ = blocks_ref.shape
    own = own_ref.shape[1]
    slab = b // n_cols
    leaf_rows = out_ref.shape[1] - own

    @pl.when(step == 0)
    def _():
        for t in range(parts.shape[0]):
            high, low = split(tops_ref[t])
            parts[t, :own] = high
            parts[t, own:] = low
        for c in range(n_cols):
            out_ref[c, leaf_rows:] = tops_ref[row_ref[0]]

    results = []
    for i in range(count):
        leaf = step * count + i
        both = jnp.concatenate([parts[targets_ref[p, leaf]] for p in range(n_cols)], axis=1)
        high, low = split(blocks_ref[:, i].reshape(n_cols * b, b))
        r = dot(both, high)
        left = own_ref[i] - ((r[:own] + r[own:]) + dot(both[:own], low))
        results.append(dot3(left, inv_ref[:, i].reshape(b, b)))
    turned = jnp.concatenate(results, axis=0).T
    for c in range(n_cols):
        out_ref[c, pl.ds(pl.multiple_of(step * slab, slab), slab)] = turned[
            c * slab : (c + 1) * slab
        ]


def leaf_backward(row, targets, tops, blocks, own, inv):
    n_cols, leaves, b, _ = blocks.shape
    mine = own.shape[1]
    slab = b // n_cols
    step = b // mine
    out = (n_cols, leaves // step * slab + mine, b)
    return pl.pallas_call(
        leaf_backward_kernel,
        grid_spec=pltpu.PrefetchScalarGridSpec(
            num_scalar_prefetch=2,
            grid=(leaves // step,),
            in_specs=[
                whole(tops.shape),
                pl.BlockSpec((n_cols, step, b, b), lambda i, *_: (0, i, 0, 0)),
                pl.BlockSpec((step, mine, b), lambda i, *_: (i, 0, 0)),
                pl.BlockSpec((n_cols, step, slab, b), lambda i, *_: (0, i, 0, 0)),
            ],
            out_specs=whole(out),
            scratch_shapes=[pltpu.VMEM((tops.shape[0], 2 * mine, b), BF16)],
        ),
        out_shape=jax.ShapeDtypeStruct(out, F32),
        name="leaf_backward",
    )(row, targets, tops, blocks, own, inv)


def arrange_kernel(got_ref, leaf_ref, top_ref):
    n_cols, _, b = got_ref.shape
    leaves, slab, r = leaf_ref.shape
    own = r // n_cols
    step = b // own
    groups = leaves // step
    for h in range(2):
        for g in range(groups):
            for i in range(step):
                leaf_ref[g * step + i, :, h * b : (h + 1) * b] = jnp.concatenate(
                    [
                        got_ref[2 * q + h, g * slab : (g + 1) * slab, i * own : (i + 1) * own]
                        for q in range(step)
                    ],
                    axis=1,
                )
        top_ref[0, :, h * b : (h + 1) * b] = jnp.concatenate(
            [got_ref[2 * q + h, groups * slab :] for q in range(step)], axis=0
        ).T


def arrange(got, leaves, r):
    n_cols, _, b = got.shape
    return pl.pallas_call(
        arrange_kernel,
        out_shape=[
            jax.ShapeDtypeStruct((leaves, b // n_cols, r), F32),
            jax.ShapeDtypeStruct((1, b, r), F32),
        ],
        name="arrange",
    )(got)


def spread(x, axis):
    n = lax.axis_size(axis)
    return lax.all_to_all(jnp.broadcast_to(x, (n,) + x.shape), axis, 0, 0, tiled=True)


def from_core(x):
    return lax.ppermute(x, "core", [(0, 1), (1, 0)])


def on_device(known, pivot, leaf_blocks, leaf_target, top_rhs, top_inv, top_sub):
    leaves, b, r = known.shape
    n_y = lax.axis_size("y")
    n_cols = 2 * n_y
    tops = lax.axis_size(ROWS)
    y = lax.axis_index("y")
    core = lax.axis_index("core")
    row = lax.axis_index(ROWS)
    blocks = leaf_blocks[:, 0]
    slab = pivot.shape[1]
    own = r // n_cols

    all_blocks = lax.all_gather(blocks, COLS, axis=0, tiled=False)
    paired = from_core(blocks)
    named = jnp.zeros((1, slab, b), F32).at[0, 0, :leaves].set(leaf_target[:, 0].astype(F32))
    inv = spread(jnp.concatenate([pivot, named]), COLS)
    targets = inv[:, leaves, 0, :leaves].astype(jnp.int32)
    two = jnp.stack([leaf_target[:, 0], lax.dynamic_index_in_dim(targets, 2 * y + 1 - core, 0, False)])

    sums, own_forward = leaf_forward(jnp.stack([core, y]), two, inv, blocks, paired, known, tops)
    arrived = lax.all_to_all(sums, ("y", "layers"), 0, 0, tiled=True)
    own_map = top_map(top_inv, top_sub)

    own_map, sums = lax.optimization_barrier((own_map, sums))
    some_maps = lax.all_gather(own_map, "rhi", axis=0, tiled=False)
    arrived, some_maps, all_blocks = lax.optimization_barrier((arrived, some_maps, all_blocks))
    maps = lax.all_gather(some_maps, "rlo", axis=0, tiled=False)

    start = core * (r // 2) + y * own + lax.axis_index("layers") * 8
    rhs_t = lax.dynamic_slice_in_dim(top_rhs[0], start, 8, 1).T
    mine = (jnp.arange(tops) == row)[:, None, None]
    partial = jnp.where(mine, rhs_t[None], 0.0) - arrived.sum(0)

    quarter = lax.all_to_all(partial, "rlo", 0, 0, tiled=True)
    quarter = quarter.reshape((lax.axis_size("rlo"), -1) + quarter.shape[1:]).sum(0)
    quarter = spread(quarter, "rhi").sum(0)
    rhs = spread(quarter, ("rlo", "layers"))
    rhs = rhs.reshape((lax.axis_size("rlo"), -1) + rhs.shape[1:])

    own_tops = top_chain(rhs, maps)
    turned = leaf_backward(row[None], targets, own_tops, all_blocks, own_forward, inv)
    got = lax.all_to_all(turned, COLS, 0, 0, tiled=True)
    return tuple(arrange(got, leaves, r))


def solution(mesh):
    rows = mesh.shape["rows"]
    low = 4
    fine = Mesh(
        mesh.devices.reshape(
            rows // low, low, mesh.shape["cols"] // 2, 2, mesh.shape["layers"]
        ),
        ROWS + COLS + ("layers",),
    )
    held = ROWS + ("layers",)
    in_specs = (
        P(held, None, None),
        P(held, COLS, None),
        P(held, COLS, None, None),
        P(held, COLS),
        P(ROWS, None, None),
        P(ROWS, None, None),
        P(ROWS, None, None),
    )
    out_specs = (P(held, COLS, None), P(ROWS, None, None))
    return jax.shard_map(
        on_device, mesh=fine, in_specs=in_specs, out_specs=out_specs, check_vma=False
    )
```

```python
import jax
import jax.numpy as jnp
from jax import lax
from jax.experimental import pallas as pl
from jax.experimental.pallas import tpu as pltpu
from jax.sharding import Mesh, PartitionSpec as P

F32 = jnp.float32
BF16 = jnp.bfloat16
ROWS = ("rhi", "rlo")
COLS = ("y", "core")
STEP = 4


def dot(a, b, cb=0):
    return lax.dot_general(a, b, (((1,), (cb,)), ((), ())), preferred_element_type=F32)


def split(x):
    high = x.astype(BF16)
    low = (x - high.astype(F32)).astype(BF16)
    return high, low


def dot3(a, b, cb=0):
    ah, al = split(a)
    bh, bl = split(b)
    both = dot(
        jnp.concatenate([ah, al], axis=1), jnp.concatenate([bh, bh], axis=cb), cb
    )
    return both + dot(ah, bl, cb)


def row_dot(x, matrix, cb=0):
    n = x.shape[0]
    m = matrix.shape[1 - cb]
    rows = jnp.concatenate(split(x), axis=0)
    r = dot(rows, jnp.concatenate(split(matrix), axis=1 - cb), cb)
    return (r[:n, :m] + (r[n:, :m] + r[:n, m:])) + r[n:, m:]


def whole(shape):
    return pl.BlockSpec(shape, lambda *_: (0,) * len(shape))


def leaf_forward_kernel(place_ref, targets_ref, inv_ref, mine_ref, pair_ref, known_ref, sums_ref, own_ref, stage):
    step = pl.program_id(0)
    count, b = mine_ref.shape[:2]
    own = own_ref.shape[1]

    @pl.when(step == 0)
    def _():
        sums_ref[...] = jnp.zeros_like(sums_ref)

    for i in range(count):
        inv = inv_ref[:, i].reshape(b, b)
        forward = dot3(known_ref[i].T, inv, 1)
        update = dot3(forward, jnp.concatenate([mine_ref[i], pair_ref[i]], axis=0), 1)
        for k in range(2):
            t = targets_ref[k, step * count + i]
            for q in range(sums_ref.shape[0]):
                sums_ref[q, t] += update[8 * q : 8 * q + 8, k * b : (k + 1) * b]
        stage[i] = forward
        own_ref[i] = stage[i, pl.ds(pl.multiple_of(place_ref[1] * own, own), own), :]


def leaf_forward(place, targets, inv, mine, pair, known, tops):
    leaves, b, r = known.shape
    n_cols, _, slab, _ = inv.shape
    half = r // 2
    own = r // n_cols
    block = pl.BlockSpec((STEP, b, b), lambda i, *_: (i, 0, 0))
    return pl.pallas_call(
        leaf_forward_kernel,
        grid_spec=pltpu.PrefetchScalarGridSpec(
            num_scalar_prefetch=2,
            grid=(leaves // STEP,),
            in_specs=[
                pl.BlockSpec((n_cols, STEP, slab, b), lambda i, *_: (0, i, 0, 0)),
                block,
                block,
                pl.BlockSpec((STEP, b, half), lambda i, place, _: (i, 0, place[0])),
            ],
            out_specs=[
                whole((half // 8, tops, 8, b)),
                pl.BlockSpec((STEP, own, b), lambda i, *_: (i, 0, 0)),
            ],
            scratch_shapes=[pltpu.VMEM((STEP, half, b), F32)],
        ),
        out_shape=[
            jax.ShapeDtypeStruct((half // 8, tops, 8, b), F32),
            jax.ShapeDtypeStruct((leaves, own, b), F32),
        ],
        name="leaf_forward",
    )(place, targets, inv, mine, pair, known)


def top_map_kernel(inv_ref, sub_ref, out_ref):
    out_ref[0] = inv_ref[0]
    out_ref[1] = -lax.dot_general(
        inv_ref[0],
        sub_ref[0],
        (((1,), (0,)), ((), ())),
        precision=lax.Precision.HIGHEST,
        preferred_element_type=F32,
    )


def top_map(inv, sub):
    return pl.pallas_call(
        top_map_kernel,
        out_shape=jax.ShapeDtypeStruct((2,) + inv.shape[1:], F32),
        name="top_map",
    )(inv, sub)


def top_chain_kernel(rhs_ref, maps_ref, out_ref):
    low, layers, high, n, b = rhs_ref.shape
    tops = low * high

    def rhs(t):
        return rhs_ref[t // high, :, t % high].reshape(layers * n, b)

    def maps(t, kind):
        return maps_ref[t, kind]

    solved = []
    current = row_dot(rhs(0), maps(0, 0), 1)
    solved.append(current)
    for t in range(1, tops):
        current = row_dot(rhs(t), maps(t, 0), 1) + row_dot(current, maps(t, 1), 1)
        solved.append(current)
    rest = solved[tops - 1]
    out_ref[tops - 1] = row_dot(rest, maps(tops - 1, 0))
    for t in range(tops - 2, -1, -1):
        rest = solved[t] + row_dot(rest, maps(t + 1, 1))
        out_ref[t] = row_dot(rest, maps(t, 0))


def top_chain(rhs, maps):
    low, layers, high, n, b = rhs.shape
    return pl.pallas_call(
        top_chain_kernel,
        out_shape=jax.ShapeDtypeStruct((low * high, layers * n, b), F32),
        name="top_chain",
    )(rhs, maps)


def leaf_backward_kernel(row_ref, targets_ref, tops_ref, *refs):
    *block_refs, own_ref, inv_ref, out_ref, parts = refs
    step = pl.program_id(0)
    n_cols = len(block_refs)
    count, b, _ = block_refs[0].shape
    own = own_ref.shape[1]
    slab = b // n_cols
    leaf_rows = out_ref.shape[1] - own

    @pl.when(step == 0)
    def _():
        for t in range(parts.shape[0]):
            high, low = split(tops_ref[t])
            parts[t, :own] = high
            parts[t, own:] = low
        for c in range(n_cols):
            out_ref[c, leaf_rows:] = tops_ref[row_ref[0]]

    results = []
    for i in range(count):
        leaf = step * count + i
        both = jnp.concatenate([parts[targets_ref[p, leaf]] for p in range(n_cols)], axis=1)
        high, low = split(jnp.concatenate([ref[i] for ref in block_refs], axis=0))
        r = dot(both, high)
        left = own_ref[i] - ((r[:own] + r[own:]) + dot(both[:own], low))
        results.append(dot3(left, inv_ref[:, i].reshape(b, b)))
    turned = jnp.concatenate(results, axis=0).T
    for c in range(n_cols):
        out_ref[c, pl.ds(pl.multiple_of(step * slab, slab), slab)] = turned[
            c * slab : (c + 1) * slab
        ]


def leaf_backward(row, targets, tops, blocks, own, inv):
    n_cols = len(blocks)
    leaves, b, _ = blocks[0].shape
    mine = own.shape[1]
    slab = b // n_cols
    step = b // mine
    out = (n_cols, leaves // step * slab + mine, b)
    return pl.pallas_call(
        leaf_backward_kernel,
        grid_spec=pltpu.PrefetchScalarGridSpec(
            num_scalar_prefetch=2,
            grid=(leaves // step,),
            in_specs=[whole(tops.shape)]
            + [pl.BlockSpec((step, b, b), lambda i, *_: (i, 0, 0))] * n_cols
            + [
                pl.BlockSpec((step, mine, b), lambda i, *_: (i, 0, 0)),
                pl.BlockSpec((n_cols, step, slab, b), lambda i, *_: (0, i, 0, 0)),
            ],
            out_specs=whole(out),
            scratch_shapes=[pltpu.VMEM((tops.shape[0], 2 * mine, b), BF16)],
        ),
        out_shape=jax.ShapeDtypeStruct(out, F32),
        name="leaf_backward",
    )(row, targets, tops, *blocks, own, inv)


def arrange_kernel(got_ref, leaf_ref, top_ref):
    n_cols, _, b = got_ref.shape
    leaves, slab, r = leaf_ref.shape
    own = r // n_cols
    step = b // own
    groups = leaves // step
    for h in range(2):
        for g in range(groups):
            for i in range(step):
                leaf_ref[g * step + i, :, h * b : (h + 1) * b] = jnp.concatenate(
                    [
                        got_ref[2 * q + h, g * slab : (g + 1) * slab, i * own : (i + 1) * own]
                        for q in range(step)
                    ],
                    axis=1,
                )
        top_ref[0, :, h * b : (h + 1) * b] = jnp.concatenate(
            [got_ref[2 * q + h, groups * slab :] for q in range(step)], axis=0
        ).T


def arrange(got, leaves, r):
    n_cols, _, b = got.shape
    return pl.pallas_call(
        arrange_kernel,
        out_shape=[
            jax.ShapeDtypeStruct((leaves, b // n_cols, r), F32),
            jax.ShapeDtypeStruct((1, b, r), F32),
        ],
        name="arrange",
    )(got)


def spread(x, axis):
    n = lax.axis_size(axis)
    return lax.all_to_all(jnp.broadcast_to(x, (n,) + x.shape), axis, 0, 0, tiled=True)


def from_core(x):
    return lax.ppermute(x, "core", [(0, 1), (1, 0)])


def from_y(x, step):
    n = lax.axis_size("y")
    return lax.ppermute(x, "y", [(i, (i - step) % n) for i in range(n)])


def on_device(known, pivot, leaf_blocks, leaf_target, top_rhs, top_inv, top_sub):
    leaves, b, r = known.shape
    n_y = lax.axis_size("y")
    n_cols = 2 * n_y
    tops = lax.axis_size(ROWS)
    y = lax.axis_index("y")
    core = lax.axis_index("core")
    row = lax.axis_index(ROWS)
    blocks = leaf_blocks[:, 0]
    slab = pivot.shape[1]
    own = r // n_cols

    named = jnp.zeros((1, slab, b), F32).at[0, 0, :leaves].set(leaf_target[:, 0].astype(F32))
    packed = jnp.concatenate([pivot, named])
    inv = spread(packed, COLS)
    maps = lax.all_gather(top_map(top_inv, top_sub), ROWS, axis=0, tiled=False)
    paired = from_core(blocks)
    far = [from_y(blocks, step) for step in range(1, n_y)]

    targets = inv[:, leaves, 0, :leaves].astype(jnp.int32).reshape(n_y, 2, leaves)
    targets = jnp.roll(targets, -y, axis=0)
    targets = jnp.where(core == 0, targets, targets[:, ::-1]).reshape(n_cols, leaves)

    sums, own_forward = leaf_forward(jnp.stack([core, y]), targets, inv, blocks, paired, known, tops)
    arrived = lax.all_to_all(sums, ("y", "layers"), 0, 0, tiled=True)

    start = core * (r // 2) + y * own + lax.axis_index("layers") * 8
    rhs_t = lax.dynamic_slice_in_dim(top_rhs[0], start, 8, 1).T
    mine = (jnp.arange(tops) == row)[:, None, None]
    partial = jnp.where(mine, rhs_t[None], 0.0) - arrived.sum(0)

    quarter = lax.all_to_all(partial, "rlo", 0, 0, tiled=True)
    quarter = quarter.reshape((lax.axis_size("rlo"), -1) + quarter.shape[1:]).sum(0)
    quarter = spread(quarter, "rhi").sum(0)
    quarter, far = lax.optimization_barrier((quarter, far))
    all_blocks = [blocks, paired]
    for block in far:
        all_blocks += [block, from_core(block)]
    rhs = spread(quarter, ("rlo", "layers"))
    rhs = rhs.reshape((lax.axis_size("rlo"), -1) + rhs.shape[1:])

    own_tops = top_chain(rhs, maps)
    turned = leaf_backward(row[None], targets, own_tops, all_blocks, own_forward, inv)
    got = lax.all_to_all(turned, COLS, 0, 0, tiled=True)
    return tuple(arrange(got, leaves, r))


def solution(mesh):
    rows = mesh.shape["rows"]
    low = 4
    fine = Mesh(
        mesh.devices.reshape(
            rows // low, low, mesh.shape["cols"] // 2, 2, mesh.shape["layers"]
        ),
        ROWS + COLS + ("layers",),
    )
    held = ROWS + ("layers",)
    in_specs = (
        P(held, None, None),
        P(held, COLS, None),
        P(held, COLS, None, None),
        P(held, COLS),
        P(ROWS, None, None),
        P(ROWS, None, None),
        P(ROWS, None, None),
    )
    out_specs = (P(held, COLS, None), P(ROWS, None, None))
    return jax.shard_map(
        on_device, mesh=fine, in_specs=in_specs, out_specs=out_specs, check_vma=False
    )
```

```python
import jax
import jax.numpy as jnp
from jax import lax
from jax.experimental import pallas as pl
from jax.experimental.pallas import tpu as pltpu
from jax.sharding import Mesh, PartitionSpec as P

F32 = jnp.float32
BF16 = jnp.bfloat16
ROWS = ("rhi", "rlo")
COLS = ("y", "core")
STEP = 4


def dot(a, b, cb=0):
    return lax.dot_general(a, b, (((1,), (cb,)), ((), ())), preferred_element_type=F32)


def split(x):
    high = x.astype(BF16)
    low = (x - high.astype(F32)).astype(BF16)
    return high, low


def dot3(a, b, cb=0):
    ah, al = split(a)
    bh, bl = split(b)
    both = dot(
        jnp.concatenate([ah, al], axis=1), jnp.concatenate([bh, bh], axis=cb), cb
    )
    return both + dot(ah, bl, cb)


def row_dot(x, matrix, cb=0):
    n = x.shape[0]
    m = matrix.shape[1 - cb]
    rows = jnp.concatenate(split(x), axis=0)
    r = dot(rows, jnp.concatenate(split(matrix), axis=1 - cb), cb)
    return (r[:n, :m] + (r[n:, :m] + r[:n, m:])) + r[n:, m:]


def whole(shape):
    return pl.BlockSpec(shape, lambda *_: (0,) * len(shape))


def leaf_forward_kernel(place_ref, targets_ref, inv_ref, mine_ref, pair_ref, known_ref, sums_ref, own_ref, stage):
    step = pl.program_id(0)
    count, b = mine_ref.shape[:2]
    own = own_ref.shape[1]

    @pl.when(step == 0)
    def _():
        sums_ref[...] = jnp.zeros_like(sums_ref)

    for i in range(count):
        inv = inv_ref[:, i].reshape(b, b)
        forward = dot3(known_ref[i].T, inv, 1)
        update = dot3(forward, jnp.concatenate([mine_ref[i], pair_ref[i]], axis=0), 1)
        for k in range(2):
            t = targets_ref[k, step * count + i]
            for q in range(sums_ref.shape[0]):
                sums_ref[q, t] += update[8 * q : 8 * q + 8, k * b : (k + 1) * b]
        stage[i] = forward
        own_ref[i] = stage[i, pl.ds(pl.multiple_of(place_ref[1] * own, own), own), :]


def leaf_forward(place, targets, inv, mine, pair, known, tops):
    leaves, b, r = known.shape
    n_cols, _, slab, _ = inv.shape
    half = r // 2
    own = r // n_cols
    block = pl.BlockSpec((STEP, b, b), lambda i, *_: (i, 0, 0))
    return pl.pallas_call(
        leaf_forward_kernel,
        grid_spec=pltpu.PrefetchScalarGridSpec(
            num_scalar_prefetch=2,
            grid=(leaves // STEP,),
            in_specs=[
                pl.BlockSpec((n_cols, STEP, slab, b), lambda i, *_: (0, i, 0, 0)),
                block,
                block,
                pl.BlockSpec((STEP, b, half), lambda i, place, _: (i, 0, place[0])),
            ],
            out_specs=[
                whole((half // 8, tops, 8, b)),
                pl.BlockSpec((STEP, own, b), lambda i, *_: (i, 0, 0)),
            ],
            scratch_shapes=[pltpu.VMEM((STEP, half, b), F32)],
        ),
        out_shape=[
            jax.ShapeDtypeStruct((half // 8, tops, 8, b), F32),
            jax.ShapeDtypeStruct((leaves, own, b), F32),
        ],
        name="leaf_forward",
    )(place, targets, inv, mine, pair, known)


def top_map_kernel(inv_ref, sub_ref, out_ref):
    out_ref[0] = inv_ref[0]
    out_ref[1] = -lax.dot_general(
        inv_ref[0],
        sub_ref[0],
        (((1,), (0,)), ((), ())),
        precision=lax.Precision.HIGHEST,
        preferred_element_type=F32,
    )


def top_map(inv, sub):
    return pl.pallas_call(
        top_map_kernel,
        out_shape=jax.ShapeDtypeStruct((2,) + inv.shape[1:], F32),
        name="top_map",
    )(inv, sub)


def top_chain_kernel(rhs_ref, maps_ref, out_ref):
    low, layers, high, n, b = rhs_ref.shape
    tops = low * high

    def rhs(t):
        return rhs_ref[t // high, :, t % high].reshape(layers * n, b)

    def maps(t, kind):
        return maps_ref[t, kind]

    solved = []
    current = row_dot(rhs(0), maps(0, 0), 1)
    solved.append(current)
    for t in range(1, tops):
        current = row_dot(rhs(t), maps(t, 0), 1) + row_dot(current, maps(t, 1), 1)
        solved.append(current)
    rest = solved[tops - 1]
    out_ref[tops - 1] = row_dot(rest, maps(tops - 1, 0))
    for t in range(tops - 2, -1, -1):
        rest = solved[t] + row_dot(rest, maps(t + 1, 1))
        out_ref[t] = row_dot(rest, maps(t, 0))


def top_chain(rhs, maps):
    low, layers, high, n, b = rhs.shape
    return pl.pallas_call(
        top_chain_kernel,
        out_shape=jax.ShapeDtypeStruct((low * high, layers * n, b), F32),
        name="top_chain",
    )(rhs, maps)


def leaf_backward_kernel(row_ref, targets_ref, tops_ref, *refs):
    *block_refs, own_ref, inv_ref, out_ref, parts = refs
    step = pl.program_id(0)
    n_cols = len(block_refs)
    count, b, _ = block_refs[0].shape
    own = own_ref.shape[1]
    slab = b // n_cols
    leaf_rows = out_ref.shape[1] - own

    @pl.when(step == 0)
    def _():
        for t in range(parts.shape[0]):
            high, low = split(tops_ref[t])
            parts[t, :own] = high
            parts[t, own:] = low
        for c in range(n_cols):
            out_ref[c, leaf_rows:] = tops_ref[row_ref[0]]

    results = []
    for i in range(count):
        leaf = step * count + i
        both = jnp.concatenate([parts[targets_ref[p, leaf]] for p in range(n_cols)], axis=1)
        high, low = split(jnp.concatenate([ref[i] for ref in block_refs], axis=0))
        r = dot(both, high)
        left = own_ref[i] - ((r[:own] + r[own:]) + dot(both[:own], low))
        results.append(dot3(left, inv_ref[:, i].reshape(b, b)))
    turned = jnp.concatenate(results, axis=0).T
    for c in range(n_cols):
        out_ref[c, pl.ds(pl.multiple_of(step * slab, slab), slab)] = turned[
            c * slab : (c + 1) * slab
        ]


def leaf_backward(row, targets, tops, blocks, own, inv):
    n_cols = len(blocks)
    leaves, b, _ = blocks[0].shape
    mine = own.shape[1]
    slab = b // n_cols
    step = b // mine
    out = (n_cols, leaves // step * slab + mine, b)
    return pl.pallas_call(
        leaf_backward_kernel,
        grid_spec=pltpu.PrefetchScalarGridSpec(
            num_scalar_prefetch=2,
            grid=(leaves // step,),
            in_specs=[whole(tops.shape)]
            + [pl.BlockSpec((step, b, b), lambda i, *_: (i, 0, 0))] * n_cols
            + [
                pl.BlockSpec((step, mine, b), lambda i, *_: (i, 0, 0)),
                pl.BlockSpec((n_cols, step, slab, b), lambda i, *_: (0, i, 0, 0)),
            ],
            out_specs=whole(out),
            scratch_shapes=[pltpu.VMEM((tops.shape[0], 2 * mine, b), BF16)],
        ),
        out_shape=jax.ShapeDtypeStruct(out, F32),
        name="leaf_backward",
    )(row, targets, tops, *blocks, own, inv)


def arrange_kernel(got_ref, leaf_ref, top_ref):
    n_cols, _, b = got_ref.shape
    leaves, slab, r = leaf_ref.shape
    own = r // n_cols
    step = b // own
    groups = leaves // step
    for h in range(2):
        for g in range(groups):
            for i in range(step):
                leaf_ref[g * step + i, :, h * b : (h + 1) * b] = jnp.concatenate(
                    [
                        got_ref[2 * q + h, g * slab : (g + 1) * slab, i * own : (i + 1) * own]
                        for q in range(step)
                    ],
                    axis=1,
                )
        top_ref[0, :, h * b : (h + 1) * b] = jnp.concatenate(
            [got_ref[2 * q + h, groups * slab :] for q in range(step)], axis=0
        ).T


def arrange(got, leaves, r):
    n_cols, _, b = got.shape
    return pl.pallas_call(
        arrange_kernel,
        out_shape=[
            jax.ShapeDtypeStruct((leaves, b // n_cols, r), F32),
            jax.ShapeDtypeStruct((1, b, r), F32),
        ],
        name="arrange",
    )(got)


def spread(x, axis):
    n = lax.axis_size(axis)
    return lax.all_to_all(jnp.broadcast_to(x, (n,) + x.shape), axis, 0, 0, tiled=True)


def from_core(x):
    return lax.ppermute(x, "core", [(0, 1), (1, 0)])


def from_y(x, step):
    n = lax.axis_size("y")
    return lax.ppermute(x, "y", [(i, (i - step) % n) for i in range(n)])


def on_device(known, pivot, leaf_blocks, leaf_target, top_rhs, top_inv, top_sub):
    leaves, b, r = known.shape
    n_y = lax.axis_size("y")
    n_cols = 2 * n_y
    tops = lax.axis_size(ROWS)
    y = lax.axis_index("y")
    core = lax.axis_index("core")
    row = lax.axis_index(ROWS)
    blocks = leaf_blocks[:, 0]
    slab = pivot.shape[1]
    own = r // n_cols

    named = jnp.zeros((1, slab, b), F32).at[0, 0, :leaves].set(leaf_target[:, 0].astype(F32))
    packed = jnp.concatenate([pivot, named])
    inv = spread(packed, COLS)
    maps = lax.all_gather(top_map(top_inv, top_sub), ROWS, axis=0, tiled=False)
    paired = from_core(blocks)
    far = [from_y(blocks, 1), None, from_y(blocks, 3)]

    targets = inv[:, leaves, 0, :leaves].astype(jnp.int32).reshape(n_y, 2, leaves)
    targets = jnp.roll(targets, -y, axis=0)
    targets = jnp.where(core == 0, targets, targets[:, ::-1]).reshape(n_cols, leaves)

    sums, own_forward = leaf_forward(jnp.stack([core, y]), targets, inv, blocks, paired, known, tops)
    arrived = lax.all_to_all(sums, ("y", "layers"), 0, 0, tiled=True)

    start = core * (r // 2) + y * own + lax.axis_index("layers") * 8
    rhs_t = lax.dynamic_slice_in_dim(top_rhs[0], start, 8, 1).T
    mine = (jnp.arange(tops) == row)[:, None, None]
    partial = jnp.where(mine, rhs_t[None], 0.0) - arrived.sum(0)

    quarter = lax.all_to_all(partial, "rlo", 0, 0, tiled=True)
    quarter = quarter.reshape((lax.axis_size("rlo"), -1) + quarter.shape[1:]).sum(0)
    held, quarter = lax.optimization_barrier((blocks, quarter))
    far[1] = from_y(held, 2)
    quarter = spread(quarter, "rhi").sum(0)
    quarter, far[0], far[2] = lax.optimization_barrier((quarter, far[0], far[2]))
    all_blocks = [blocks, paired]
    for block in far:
        all_blocks += [block, from_core(block)]
    rhs = spread(quarter, ("rlo", "layers"))
    rhs = rhs.reshape((lax.axis_size("rlo"), -1) + rhs.shape[1:])

    own_tops = top_chain(rhs, maps)
    turned = leaf_backward(row[None], targets, own_tops, all_blocks, own_forward, inv)
    got = lax.all_to_all(turned, COLS, 0, 0, tiled=True)
    return tuple(arrange(got, leaves, r))


def solution(mesh):
    rows = mesh.shape["rows"]
    low = 4
    fine = Mesh(
        mesh.devices.reshape(
            rows // low, low, mesh.shape["cols"] // 2, 2, mesh.shape["layers"]
        ),
        ROWS + COLS + ("layers",),
    )
    held = ROWS + ("layers",)
    in_specs = (
        P(held, None, None),
        P(held, COLS, None),
        P(held, COLS, None, None),
        P(held, COLS),
        P(ROWS, None, None),
        P(ROWS, None, None),
        P(ROWS, None, None),
    )
    out_specs = (P(held, COLS, None), P(ROWS, None, None))
    return jax.shard_map(
        on_device, mesh=fine, in_specs=in_specs, out_specs=out_specs, check_vma=False
    )
```

```python
import jax
import jax.numpy as jnp
from jax import lax
from jax.experimental import pallas as pl
from jax.experimental.pallas import tpu as pltpu
from jax.sharding import Mesh, PartitionSpec as P

F32 = jnp.float32
BF16 = jnp.bfloat16
ROWS = ("rhi", "rlo")
COLS = ("y", "core")
STEP = 4


def dot(a, b, cb=0):
    return lax.dot_general(a, b, (((1,), (cb,)), ((), ())), preferred_element_type=F32)


def split(x):
    high = x.astype(BF16)
    low = (x - high.astype(F32)).astype(BF16)
    return high, low


def dot3(a, b, cb=0):
    ah, al = split(a)
    bh, bl = split(b)
    both = dot(
        jnp.concatenate([ah, al], axis=1), jnp.concatenate([bh, bh], axis=cb), cb
    )
    return both + dot(ah, bl, cb)


def row_dot(x, matrix, cb=0):
    n = x.shape[0]
    m = matrix.shape[1 - cb]
    rows = jnp.concatenate(split(x), axis=0)
    r = dot(rows, jnp.concatenate(split(matrix), axis=1 - cb), cb)
    return (r[:n, :m] + (r[n:, :m] + r[:n, m:])) + r[n:, m:]


def whole(shape):
    return pl.BlockSpec(shape, lambda *_: (0,) * len(shape))


def prepare_kernel(targets_ref, pivot_ref, inv_ref, sub_ref, out_ref, maps_ref):
    leaves, slab, b = pivot_ref.shape
    line = lax.broadcasted_iota(jnp.int32, (slab, b), 0)
    named = jnp.zeros((slab, b), F32)
    for i in range(leaves):
        named = jnp.where(line == i, targets_ref[i].astype(F32), named)
    for c in range(out_ref.shape[0]):
        out_ref[c, :leaves] = pivot_ref[...]
        out_ref[c, leaves] = named
    maps_ref[0] = inv_ref[0]
    maps_ref[1] = -lax.dot_general(
        inv_ref[0],
        sub_ref[0],
        (((1,), (0,)), ((), ())),
        precision=lax.Precision.HIGHEST,
        preferred_element_type=F32,
    )


def prepare(targets, pivot, inv, sub, n_cols):
    leaves, slab, b = pivot.shape
    vmem = pl.BlockSpec(memory_space=pltpu.VMEM)
    return pl.pallas_call(
        prepare_kernel,
        in_specs=[pl.BlockSpec(memory_space=pltpu.SMEM), vmem, vmem, vmem],
        out_specs=[vmem, vmem],
        out_shape=[
            jax.ShapeDtypeStruct((n_cols, leaves + 1, slab, b), F32),
            jax.ShapeDtypeStruct((2,) + inv.shape[1:], F32),
        ],
        name="prepare",
    )(targets, pivot, inv, sub)


def leaf_forward_kernel(place_ref, targets_ref, rhs_ref, inv_ref, mine_ref, pair_ref, known_ref, sums_ref, own_ref, stage):
    core, y, part, row = (place_ref[k] for k in range(4))
    step = pl.program_id(0)
    count, b = mine_ref.shape[:2]
    own = own_ref.shape[1]

    @pl.when(step == 0)
    def _():
        sums_ref[...] = jnp.zeros_like(sums_ref)
        sums_ref[part, row] = rhs_ref[...]

    for i in range(count):
        inv = inv_ref[:, i].reshape(b, b)
        forward = dot3(known_ref[i].T, inv, 1)
        update = dot3(forward, jnp.concatenate([mine_ref[i], pair_ref[i]], axis=0), 1)
        for k in range(2):
            t = targets_ref[2 * y + (core if k == 0 else 1 - core), step * count + i]
            for q in range(sums_ref.shape[0]):
                sums_ref[q, t] -= update[8 * q : 8 * q + 8, k * b : (k + 1) * b]
        stage[i] = forward
        own_ref[i] = stage[i, pl.ds(pl.multiple_of(y * own, own), own), :]


def leaf_forward(place, targets, rhs, inv, mine, pair, known, tops):
    leaves, b, r = known.shape
    n_cols, _, slab, _ = inv.shape
    half = r // 2
    own = r // n_cols
    block = pl.BlockSpec((STEP, b, b), lambda i, *_: (i, 0, 0))
    return pl.pallas_call(
        leaf_forward_kernel,
        grid_spec=pltpu.PrefetchScalarGridSpec(
            num_scalar_prefetch=2,
            grid=(leaves // STEP,),
            in_specs=[
                whole(rhs.shape),
                pl.BlockSpec((n_cols, STEP, slab, b), lambda i, *_: (0, i, 0, 0)),
                block,
                block,
                pl.BlockSpec((STEP, b, half), lambda i, place, _: (i, 0, place[0])),
            ],
            out_specs=[
                whole((half // 8, tops, 8, b)),
                pl.BlockSpec((STEP, own, b), lambda i, *_: (i, 0, 0)),
            ],
            scratch_shapes=[pltpu.VMEM((STEP, half, b), F32)],
        ),
        out_shape=[
            jax.ShapeDtypeStruct((half // 8, tops, 8, b), F32),
            jax.ShapeDtypeStruct((leaves, own, b), F32),
        ],
        name="leaf_forward",
    )(place, targets, rhs, inv, mine, pair, known)


def top_chain_kernel(rhs_ref, maps_ref, out_ref):
    low, layers, high, n, b = rhs_ref.shape
    tops = low * high

    def rhs(t):
        return rhs_ref[t // high, :, t % high].reshape(layers * n, b)

    def maps(t, kind):
        return maps_ref[t, kind]

    solved = []
    current = row_dot(rhs(0), maps(0, 0), 1)
    solved.append(current)
    for t in range(1, tops):
        current = row_dot(rhs(t), maps(t, 0), 1) + row_dot(current, maps(t, 1), 1)
        solved.append(current)
    rest = solved[tops - 1]
    out_ref[tops - 1] = row_dot(rest, maps(tops - 1, 0))
    for t in range(tops - 2, -1, -1):
        rest = solved[t] + row_dot(rest, maps(t + 1, 1))
        out_ref[t] = row_dot(rest, maps(t, 0))


def top_chain(rhs, maps):
    low, layers, high, n, b = rhs.shape
    return pl.pallas_call(
        top_chain_kernel,
        out_shape=jax.ShapeDtypeStruct((low * high, layers * n, b), F32),
        name="top_chain",
    )(rhs, maps)


def leaf_backward_kernel(place_ref, targets_ref, tops_ref, *refs):
    *block_refs, own_ref, inv_ref, out_ref, parts = refs
    core, y, _, row = (place_ref[k] for k in range(4))
    step = pl.program_id(0)
    n_cols = len(block_refs)
    count, b, _ = block_refs[0].shape
    own = own_ref.shape[1]
    slab = b // n_cols
    leaf_rows = out_ref.shape[1] - own

    @pl.when(step == 0)
    def _():
        for t in range(parts.shape[0]):
            high, low = split(tops_ref[t])
            parts[t, :own] = high
            parts[t, own:] = low
        for c in range(n_cols):
            out_ref[c, leaf_rows:] = tops_ref[row]

    results = []
    for i in range(count):
        leaf = step * count + i
        both = jnp.concatenate(
            [
                parts[targets_ref[2 * ((y + k // 2) % (n_cols // 2)) + (core + k) % 2, leaf]]
                for k in range(n_cols)
            ],
            axis=1,
        )
        high, low = split(jnp.concatenate([ref[i] for ref in block_refs], axis=0))
        r = dot(both, high)
        left = own_ref[i] - ((r[:own] + r[own:]) + dot(both[:own], low))
        results.append(dot3(left, inv_ref[:, i].reshape(b, b)))
    turned = jnp.concatenate(results, axis=0).T
    for c in range(n_cols):
        out_ref[c, pl.ds(pl.multiple_of(step * slab, slab), slab)] = turned[
            c * slab : (c + 1) * slab
        ]


def leaf_backward(place, targets, tops, blocks, own, inv):
    n_cols = len(blocks)
    leaves, b, _ = blocks[0].shape
    mine = own.shape[1]
    slab = b // n_cols
    step = b // mine
    out = (n_cols, leaves // step * slab + mine, b)
    return pl.pallas_call(
        leaf_backward_kernel,
        grid_spec=pltpu.PrefetchScalarGridSpec(
            num_scalar_prefetch=2,
            grid=(leaves // step,),
            in_specs=[whole(tops.shape)]
            + [pl.BlockSpec((step, b, b), lambda i, *_: (i, 0, 0))] * n_cols
            + [
                pl.BlockSpec((step, mine, b), lambda i, *_: (i, 0, 0)),
                pl.BlockSpec((n_cols, step, slab, b), lambda i, *_: (0, i, 0, 0)),
            ],
            out_specs=whole(out),
            scratch_shapes=[pltpu.VMEM((tops.shape[0], 2 * mine, b), BF16)],
        ),
        out_shape=jax.ShapeDtypeStruct(out, F32),
        name="leaf_backward",
    )(place, targets, tops, *blocks, own, inv)


def arrange_kernel(got_ref, leaf_ref, top_ref):
    n_cols, _, b = got_ref.shape
    leaves, slab, r = leaf_ref.shape
    own = r // n_cols
    step = b // own
    groups = leaves // step
    for h in range(2):
        for g in range(groups):
            for i in range(step):
                leaf_ref[g * step + i, :, h * b : (h + 1) * b] = jnp.concatenate(
                    [
                        got_ref[2 * q + h, g * slab : (g + 1) * slab, i * own : (i + 1) * own]
                        for q in range(step)
                    ],
                    axis=1,
                )
        top_ref[0, :, h * b : (h + 1) * b] = jnp.concatenate(
            [got_ref[2 * q + h, groups * slab :] for q in range(step)], axis=0
        ).T


def arrange(got, leaves, r):
    n_cols, _, b = got.shape
    return pl.pallas_call(
        arrange_kernel,
        out_shape=[
            jax.ShapeDtypeStruct((leaves, b // n_cols, r), F32),
            jax.ShapeDtypeStruct((1, b, r), F32),
        ],
        name="arrange",
    )(got)


def spread(x, axis):
    n = lax.axis_size(axis)
    return lax.all_to_all(jnp.broadcast_to(x, (n,) + x.shape), axis, 0, 0, tiled=True)


def from_core(x):
    return lax.ppermute(x, "core", [(0, 1), (1, 0)])


def from_y(x, step):
    n = lax.axis_size("y")
    return lax.ppermute(x, "y", [(i, (i - step) % n) for i in range(n)])


def on_device(known, pivot, leaf_blocks, leaf_target, top_rhs, top_inv, top_sub):
    leaves, b, r = known.shape
    n_y = lax.axis_size("y")
    n_cols = 2 * n_y
    tops = lax.axis_size(ROWS)
    y = lax.axis_index("y")
    core = lax.axis_index("core")
    row = lax.axis_index(ROWS)
    blocks = leaf_blocks[:, 0]
    slab = pivot.shape[1]
    own = r // n_cols

    packed, own_maps = prepare(leaf_target[:, 0], pivot, top_inv, top_sub, n_cols)
    inv = lax.all_to_all(packed, COLS, 0, 0, tiled=True)
    maps = lax.all_gather(own_maps, ROWS, axis=0, tiled=False)
    paired = from_core(blocks)
    far = [from_y(blocks, 1), None, from_y(blocks, 3)]
    targets = inv[:, leaves, :leaves, 0].astype(jnp.int32)

    part = y * lax.axis_size("layers") + lax.axis_index("layers")
    place = jnp.stack([core, y, part, row])
    rhs_t = lax.dynamic_slice_in_dim(top_rhs[0], core * (r // 2) + part * 8, 8, 1).T
    sums, own_forward = leaf_forward(place, targets, rhs_t, inv, blocks, paired, known, tops)
    partial = lax.all_to_all(sums, ("y", "layers"), 0, 0, tiled=True).sum(0)

    quarter = lax.all_to_all(partial, "rlo", 0, 0, tiled=True)
    quarter = quarter.reshape((lax.axis_size("rlo"), -1) + quarter.shape[1:]).sum(0)
    held, quarter = lax.optimization_barrier((blocks, quarter))
    far[1] = from_y(held, 2)
    quarter = spread(quarter, "rhi").sum(0)
    quarter, far[0], far[2] = lax.optimization_barrier((quarter, far[0], far[2]))
    all_blocks = [blocks, paired]
    for block in far:
        all_blocks += [block, from_core(block)]
    rhs = spread(quarter, ("rlo", "layers"))
    rhs = rhs.reshape((lax.axis_size("rlo"), -1) + rhs.shape[1:])

    own_tops = top_chain(rhs, maps)
    turned = leaf_backward(place, targets, own_tops, all_blocks, own_forward, inv)
    got = lax.all_to_all(turned, COLS, 0, 0, tiled=True)
    return tuple(arrange(got, leaves, r))


def solution(mesh):
    rows = mesh.shape["rows"]
    low = 4
    fine = Mesh(
        mesh.devices.reshape(
            rows // low, low, mesh.shape["cols"] // 2, 2, mesh.shape["layers"]
        ),
        ROWS + COLS + ("layers",),
    )
    held = ROWS + ("layers",)
    in_specs = (
        P(held, None, None),
        P(held, COLS, None),
        P(held, COLS, None, None),
        P(held, COLS),
        P(ROWS, None, None),
        P(ROWS, None, None),
        P(ROWS, None, None),
    )
    out_specs = (P(held, COLS, None), P(ROWS, None, None))
    return jax.shard_map(
        on_device, mesh=fine, in_specs=in_specs, out_specs=out_specs, check_vma=False
    )
```

```python
import jax
import jax.numpy as jnp
from jax import lax
from jax.experimental import pallas as pl
from jax.experimental.pallas import tpu as pltpu
from jax.sharding import Mesh, PartitionSpec as P

F32 = jnp.float32
BF16 = jnp.bfloat16
ROWS = ("rhi", "rlo")
COLS = ("y", "core")
STEP = 6


def dot(a, b, cb=0):
    return lax.dot_general(a, b, (((1,), (cb,)), ((), ())), preferred_element_type=F32)


def split(x):
    high = x.astype(BF16)
    low = (x - high.astype(F32)).astype(BF16)
    return high, low


def dot3(a, b, cb=0):
    ah, al = split(a)
    bh, bl = split(b)
    both = dot(
        jnp.concatenate([ah, al], axis=1), jnp.concatenate([bh, bh], axis=cb), cb
    )
    return both + dot(ah, bl, cb)


def row_dot(x, matrix, cb=0):
    n = x.shape[0]
    m = matrix.shape[1 - cb]
    rows = jnp.concatenate(split(x), axis=0)
    r = dot(rows, jnp.concatenate(split(matrix), axis=1 - cb), cb)
    return (r[:n, :m] + (r[n:, :m] + r[:n, m:])) + r[n:, m:]


def whole(shape):
    return pl.BlockSpec(shape, lambda *_: (0,) * len(shape))


def prepare_kernel(targets_ref, pivot_ref, inv_ref, sub_ref, out_ref, maps_ref):
    leaves, slab, b = pivot_ref.shape
    line = lax.broadcasted_iota(jnp.int32, (slab, b), 0)
    named = jnp.zeros((slab, b), F32)
    for i in range(leaves):
        named = jnp.where(line == i, targets_ref[i].astype(F32), named)
    for c in range(out_ref.shape[0]):
        out_ref[c, :leaves] = pivot_ref[...]
        out_ref[c, leaves] = named
    maps_ref[0] = inv_ref[0]
    maps_ref[1] = -lax.dot_general(
        inv_ref[0],
        sub_ref[0],
        (((1,), (0,)), ((), ())),
        precision=lax.Precision.HIGHEST,
        preferred_element_type=F32,
    )


def prepare(targets, pivot, inv, sub, n_cols):
    leaves, slab, b = pivot.shape
    vmem = pl.BlockSpec(memory_space=pltpu.VMEM)
    return pl.pallas_call(
        prepare_kernel,
        in_specs=[pl.BlockSpec(memory_space=pltpu.SMEM), vmem, vmem, vmem],
        out_specs=[vmem, vmem],
        out_shape=[
            jax.ShapeDtypeStruct((n_cols, leaves + 1, slab, b), F32),
            jax.ShapeDtypeStruct((2,) + inv.shape[1:], F32),
        ],
        name="prepare",
    )(targets, pivot, inv, sub)


def leaf_forward_kernel(place_ref, targets_ref, rhs_ref, inv_ref, mine_ref, pair_ref, known_ref, sums_ref, own_ref, stage):
    core, y, part, row = (place_ref[k] for k in range(4))
    step = pl.program_id(0)
    count, b = mine_ref.shape[:2]
    own = own_ref.shape[1]

    @pl.when(step == 0)
    def _():
        sums_ref[...] = jnp.zeros_like(sums_ref)
        sums_ref[part, row] = rhs_ref[...]

    for i in range(count):
        inv = inv_ref[:, i].reshape(b, b)
        forward = dot3(known_ref[i].T, inv, 1)
        update = dot3(forward, jnp.concatenate([mine_ref[i], pair_ref[i]], axis=0), 1)
        for k in range(2):
            t = targets_ref[2 * y + (core if k == 0 else 1 - core), step * count + i]
            for q in range(sums_ref.shape[0]):
                sums_ref[q, t] -= update[8 * q : 8 * q + 8, k * b : (k + 1) * b]
        stage[i] = forward
        own_ref[i] = stage[i, pl.ds(pl.multiple_of(y * own, own), own), :]


def leaf_forward(place, targets, rhs, inv, mine, pair, known, tops):
    leaves, b, r = known.shape
    n_cols, _, slab, _ = inv.shape
    half = r // 2
    own = r // n_cols
    block = pl.BlockSpec((STEP, b, b), lambda i, *_: (i, 0, 0))
    return pl.pallas_call(
        leaf_forward_kernel,
        grid_spec=pltpu.PrefetchScalarGridSpec(
            num_scalar_prefetch=2,
            grid=(leaves // STEP,),
            in_specs=[
                whole(rhs.shape),
                pl.BlockSpec((n_cols, STEP, slab, b), lambda i, *_: (0, i, 0, 0)),
                block,
                block,
                pl.BlockSpec((STEP, b, half), lambda i, place, _: (i, 0, place[0])),
            ],
            out_specs=[
                whole((half // 8, tops, 8, b)),
                pl.BlockSpec((STEP, own, b), lambda i, *_: (i, 0, 0)),
            ],
            scratch_shapes=[pltpu.VMEM((STEP, half, b), F32)],
        ),
        out_shape=[
            jax.ShapeDtypeStruct((half // 8, tops, 8, b), F32),
            jax.ShapeDtypeStruct((leaves, own, b), F32),
        ],
        name="leaf_forward",
    )(place, targets, rhs, inv, mine, pair, known)


def top_chain_kernel(rhs_ref, maps_ref, out_ref):
    low, layers, high, n, b = rhs_ref.shape
    tops = low * high

    def rhs(t):
        return rhs_ref[t // high, :, t % high].reshape(layers * n, b)

    def maps(t, kind):
        return maps_ref[t, kind]

    pairs = [None] + [dot3(maps(t + 1, 1), maps(t, 1)) for t in range(2, tops, 2)]
    local = [row_dot(rhs(t), maps(t, 0), 1) for t in range(tops)]
    both = [local[t + 1] + row_dot(local[t], maps(t + 1, 1), 1) for t in range(0, tops, 2)]
    odd = [both[0]]
    for k in range(1, tops // 2):
        odd.append(both[k] + row_dot(odd[-1], pairs[k], 1))
    solved = []
    for k in range(tops // 2):
        t = 2 * k
        solved.append(local[t] + row_dot(odd[k - 1], maps(t, 1), 1) if k else local[0])
        solved.append(odd[k])
    rest = [None] * tops
    rest[tops - 1] = solved[tops - 1]
    for k in range(tops // 2 - 1, 0, -1):
        ahead = solved[2 * k - 1] + row_dot(solved[2 * k], maps(2 * k, 1))
        rest[2 * k - 1] = ahead + row_dot(rest[2 * k + 1], pairs[k])
    for t in range(tops - 2, -1, -2):
        rest[t] = solved[t] + row_dot(rest[t + 1], maps(t + 1, 1))
    for t in range(tops):
        out_ref[t] = row_dot(rest[t], maps(t, 0))


def top_chain(rhs, maps):
    low, layers, high, n, b = rhs.shape
    return pl.pallas_call(
        top_chain_kernel,
        out_shape=jax.ShapeDtypeStruct((low * high, layers * n, b), F32),
        name="top_chain",
    )(rhs, maps)


def leaf_backward_kernel(place_ref, targets_ref, tops_ref, *refs):
    *block_refs, own_ref, inv_ref, out_ref, parts = refs
    core, y, _, row = (place_ref[k] for k in range(4))
    step = pl.program_id(0)
    n_cols = len(block_refs)
    count, b, _ = block_refs[0].shape
    own = own_ref.shape[1]
    slab = b // n_cols
    leaf_rows = out_ref.shape[1] - own

    @pl.when(step == 0)
    def _():
        for t in range(parts.shape[0]):
            high, low = split(tops_ref[t])
            parts[t, :own] = high
            parts[t, own:] = low
        for c in range(n_cols):
            out_ref[c, leaf_rows:] = tops_ref[row]

    results = []
    for i in range(count):
        leaf = step * count + i
        both = jnp.concatenate(
            [
                parts[targets_ref[2 * ((y + k // 2) % (n_cols // 2)) + (core + k) % 2, leaf]]
                for k in range(n_cols)
            ],
            axis=1,
        )
        high, low = split(jnp.concatenate([ref[i] for ref in block_refs], axis=0))
        r = dot(both, high)
        left = own_ref[i] - ((r[:own] + r[own:]) + dot(both[:own], low))
        results.append(dot3(left, inv_ref[:, i].reshape(b, b)))
    turned = jnp.concatenate(results, axis=0).T
    for c in range(n_cols):
        out_ref[c, pl.ds(pl.multiple_of(step * slab, slab), slab)] = turned[
            c * slab : (c + 1) * slab
        ]


def leaf_backward(place, targets, tops, blocks, own, inv):
    n_cols = len(blocks)
    leaves, b, _ = blocks[0].shape
    mine = own.shape[1]
    slab = b // n_cols
    step = b // mine
    out = (n_cols, leaves // step * slab + mine, b)
    return pl.pallas_call(
        leaf_backward_kernel,
        grid_spec=pltpu.PrefetchScalarGridSpec(
            num_scalar_prefetch=2,
            grid=(leaves // step,),
            in_specs=[whole(tops.shape)]
            + [pl.BlockSpec((step, b, b), lambda i, *_: (i, 0, 0))] * n_cols
            + [
                pl.BlockSpec((step, mine, b), lambda i, *_: (i, 0, 0)),
                pl.BlockSpec((n_cols, step, slab, b), lambda i, *_: (0, i, 0, 0)),
            ],
            out_specs=whole(out),
            scratch_shapes=[pltpu.VMEM((tops.shape[0], 2 * mine, b), BF16)],
        ),
        out_shape=jax.ShapeDtypeStruct(out, F32),
        name="leaf_backward",
    )(place, targets, tops, *blocks, own, inv)


def arrange_kernel(got_ref, leaf_ref, top_ref):
    n_cols, _, b = got_ref.shape
    leaves, slab, r = leaf_ref.shape
    own = r // n_cols
    step = b // own
    groups = leaves // step
    for h in range(2):
        for g in range(groups):
            for i in range(step):
                leaf_ref[g * step + i, :, h * b : (h + 1) * b] = jnp.concatenate(
                    [
                        got_ref[2 * q + h, g * slab : (g + 1) * slab, i * own : (i + 1) * own]
                        for q in range(step)
                    ],
                    axis=1,
                )
        top_ref[0, :, h * b : (h + 1) * b] = jnp.concatenate(
            [got_ref[2 * q + h, groups * slab :] for q in range(step)], axis=0
        ).T


def arrange(got, leaves, r):
    n_cols, _, b = got.shape
    return pl.pallas_call(
        arrange_kernel,
        out_shape=[
            jax.ShapeDtypeStruct((leaves, b // n_cols, r), F32),
            jax.ShapeDtypeStruct((1, b, r), F32),
        ],
        name="arrange",
    )(got)


def spread(x, axis):
    n = lax.axis_size(axis)
    return lax.all_to_all(jnp.broadcast_to(x, (n,) + x.shape), axis, 0, 0, tiled=True)


def from_core(x):
    return lax.ppermute(x, "core", [(0, 1), (1, 0)])


def from_y(x, step):
    n = lax.axis_size("y")
    return lax.ppermute(x, "y", [(i, (i - step) % n) for i in range(n)])


def on_device(known, pivot, leaf_blocks, leaf_target, top_rhs, top_inv, top_sub):
    leaves, b, r = known.shape
    n_y = lax.axis_size("y")
    n_cols = 2 * n_y
    tops = lax.axis_size(ROWS)
    y = lax.axis_index("y")
    core = lax.axis_index("core")
    row = lax.axis_index(ROWS)
    blocks = leaf_blocks[:, 0]
    slab = pivot.shape[1]
    own = r // n_cols

    packed, own_maps = prepare(leaf_target[:, 0], pivot, top_inv, top_sub, n_cols)
    inv = lax.all_to_all(packed, COLS, 0, 0, tiled=True)
    maps = lax.all_gather(own_maps, ROWS, axis=0, tiled=False)
    paired = from_core(blocks)
    far = [from_y(blocks, 1), None, from_y(blocks, 3)]
    targets = inv[:, leaves, :leaves, 0].astype(jnp.int32)

    part = y * lax.axis_size("layers") + lax.axis_index("layers")
    place = jnp.stack([core, y, part, row])
    rhs_t = lax.dynamic_slice_in_dim(top_rhs[0], core * (r // 2) + part * 8, 8, 1).T
    sums, own_forward = leaf_forward(place, targets, rhs_t, inv, blocks, paired, known, tops)
    partial = lax.all_to_all(sums, ("y", "layers"), 0, 0, tiled=True).sum(0)

    quarter = lax.all_to_all(partial, "rlo", 0, 0, tiled=True)
    quarter = quarter.reshape((lax.axis_size("rlo"), -1) + quarter.shape[1:]).sum(0)
    held, quarter = lax.optimization_barrier((blocks, quarter))
    far[1] = from_y(held, 2)
    quarter = spread(quarter, "rhi").sum(0)
    quarter, far[0], far[2] = lax.optimization_barrier((quarter, far[0], far[2]))
    all_blocks = [blocks, paired]
    for block in far:
        all_blocks += [block, from_core(block)]
    rhs = spread(quarter, ("rlo", "layers"))
    rhs = rhs.reshape((lax.axis_size("rlo"), -1) + rhs.shape[1:])

    own_tops = top_chain(rhs, maps)
    turned = leaf_backward(place, targets, own_tops, all_blocks, own_forward, inv)
    got = lax.all_to_all(turned, COLS, 0, 0, tiled=True)
    return tuple(arrange(got, leaves, r))


def solution(mesh):
    rows = mesh.shape["rows"]
    low = 4
    fine = Mesh(
        mesh.devices.reshape(
            rows // low, low, mesh.shape["cols"] // 2, 2, mesh.shape["layers"]
        ),
        ROWS + COLS + ("layers",),
    )
    held = ROWS + ("layers",)
    in_specs = (
        P(held, None, None),
        P(held, COLS, None),
        P(held, COLS, None, None),
        P(held, COLS),
        P(ROWS, None, None),
        P(ROWS, None, None),
        P(ROWS, None, None),
    )
    out_specs = (P(held, COLS, None), P(ROWS, None, None))
    return jax.shard_map(
        on_device, mesh=fine, in_specs=in_specs, out_specs=out_specs, check_vma=False
    )
```

```python
import jax
import jax.numpy as jnp
from jax import lax
from jax.experimental import pallas as pl
from jax.experimental.pallas import tpu as pltpu
from jax.sharding import Mesh, PartitionSpec as P

F32 = jnp.float32
BF16 = jnp.bfloat16
ROWS = ("rhi", "rlo")
COLS = ("y", "core")
STEP = 6


def dot(a, b, cb=0):
    return lax.dot_general(a, b, (((1,), (cb,)), ((), ())), preferred_element_type=F32)


def split(x):
    high = x.astype(BF16)
    low = (x - high.astype(F32)).astype(BF16)
    return high, low


def dot3(a, b, cb=0):
    ah, al = split(a)
    bh, bl = split(b)
    both = dot(
        jnp.concatenate([ah, al], axis=1), jnp.concatenate([bh, bh], axis=cb), cb
    )
    return both + dot(ah, bl, cb)


def row_dot(x, matrix, cb=0):
    n = x.shape[0]
    m = matrix.shape[1 - cb]
    rows = jnp.concatenate(split(x), axis=0)
    r = dot(rows, jnp.concatenate(split(matrix), axis=1 - cb), cb)
    return (r[:n, :m] + (r[n:, :m] + r[:n, m:])) + r[n:, m:]


def whole(shape):
    return pl.BlockSpec(shape, lambda *_: (0,) * len(shape))


def prepare_kernel(targets_ref, pivot_ref, inv_ref, sub_ref, out_ref, maps_ref):
    leaves, slab, b = pivot_ref.shape
    line = lax.broadcasted_iota(jnp.int32, (slab, b), 0)
    named = jnp.zeros((slab, b), F32)
    for i in range(leaves):
        named = jnp.where(line == i, targets_ref[i].astype(F32), named)
    for c in range(out_ref.shape[0]):
        out_ref[c, :leaves] = pivot_ref[...]
        out_ref[c, leaves] = named
    maps_ref[0] = inv_ref[0]
    maps_ref[1] = -lax.dot_general(
        inv_ref[0],
        sub_ref[0],
        (((1,), (0,)), ((), ())),
        precision=lax.Precision.HIGHEST,
        preferred_element_type=F32,
    )


def prepare(targets, pivot, inv, sub, n_cols):
    leaves, slab, b = pivot.shape
    vmem = pl.BlockSpec(memory_space=pltpu.VMEM)
    return pl.pallas_call(
        prepare_kernel,
        in_specs=[pl.BlockSpec(memory_space=pltpu.SMEM), vmem, vmem, vmem],
        out_specs=[vmem, vmem],
        out_shape=[
            jax.ShapeDtypeStruct((n_cols, leaves + 1, slab, b), F32),
            jax.ShapeDtypeStruct((2,) + inv.shape[1:], F32),
        ],
        name="prepare",
    )(targets, pivot, inv, sub)


def leaf_forward_kernel(place_ref, targets_ref, rhs_ref, inv_ref, mine_ref, pair_ref, known_ref, sums_ref, own_ref, stage):
    core, y, part, row = (place_ref[k] for k in range(4))
    step = pl.program_id(0)
    count, b = mine_ref.shape[:2]
    own = own_ref.shape[1]

    @pl.when(step == 0)
    def _():
        sums_ref[...] = jnp.zeros_like(sums_ref)
        sums_ref[part, row] = rhs_ref[...]

    for i in range(count):
        inv = inv_ref[:, i].reshape(b, b)
        forward = dot3(known_ref[i].T, inv, 1)
        update = dot3(forward, jnp.concatenate([mine_ref[i], pair_ref[i]], axis=0), 1)
        for k in range(2):
            t = targets_ref[2 * y + (core if k == 0 else 1 - core), step * count + i]
            for q in range(sums_ref.shape[0]):
                sums_ref[q, t] -= update[8 * q : 8 * q + 8, k * b : (k + 1) * b]
        stage[i] = forward
        own_ref[i] = stage[i, pl.ds(pl.multiple_of(y * own, own), own), :]


def leaf_forward(place, targets, rhs, inv, mine, pair, known, tops):
    leaves, b, r = known.shape
    n_cols, _, slab, _ = inv.shape
    half = r // 2
    own = r // n_cols
    block = pl.BlockSpec((STEP, b, b), lambda i, *_: (i, 0, 0))
    return pl.pallas_call(
        leaf_forward_kernel,
        grid_spec=pltpu.PrefetchScalarGridSpec(
            num_scalar_prefetch=2,
            grid=(leaves // STEP,),
            in_specs=[
                whole(rhs.shape),
                pl.BlockSpec((n_cols, STEP, slab, b), lambda i, *_: (0, i, 0, 0)),
                block,
                block,
                pl.BlockSpec((STEP, b, half), lambda i, place, _: (i, 0, place[0])),
            ],
            out_specs=[
                whole((half // 8, tops, 8, b)),
                pl.BlockSpec((STEP, own, b), lambda i, *_: (i, 0, 0)),
            ],
            scratch_shapes=[pltpu.VMEM((STEP, half, b), F32)],
        ),
        out_shape=[
            jax.ShapeDtypeStruct((half // 8, tops, 8, b), F32),
            jax.ShapeDtypeStruct((leaves, own, b), F32),
        ],
        name="leaf_forward",
    )(place, targets, rhs, inv, mine, pair, known)


def top_chain_kernel(rhs_ref, maps_ref, out_ref):
    low, layers, high, n, b = rhs_ref.shape
    tops = low * high

    def rhs(t):
        return rhs_ref[t // high, :, t % high].reshape(layers * n, b)

    def maps(t, kind):
        return maps_ref[t, kind]

    pairs = [None] + [dot3(maps(t + 1, 1), maps(t, 1)) for t in range(2, tops, 2)]
    local = [row_dot(rhs(t), maps(t, 0), 1) for t in range(tops)]
    both = [local[t + 1] + row_dot(local[t], maps(t + 1, 1), 1) for t in range(0, tops, 2)]
    odd = [both[0]]
    for k in range(1, tops // 2):
        odd.append(both[k] + row_dot(odd[-1], pairs[k], 1))
    solved = []
    for k in range(tops // 2):
        t = 2 * k
        solved.append(local[t] + row_dot(odd[k - 1], maps(t, 1), 1) if k else local[0])
        solved.append(odd[k])
    rest = [None] * tops
    rest[tops - 1] = solved[tops - 1]
    for k in range(tops // 2 - 1, 0, -1):
        ahead = solved[2 * k - 1] + row_dot(solved[2 * k], maps(2 * k, 1))
        rest[2 * k - 1] = ahead + row_dot(rest[2 * k + 1], pairs[k])
    for t in range(tops - 2, -1, -2):
        rest[t] = solved[t] + row_dot(rest[t + 1], maps(t + 1, 1))
    for t in range(tops):
        out_ref[t] = row_dot(rest[t], maps(t, 0))


def top_chain(rhs, maps):
    low, layers, high, n, b = rhs.shape
    return pl.pallas_call(
        top_chain_kernel,
        out_shape=jax.ShapeDtypeStruct((low * high, layers * n, b), F32),
        name="top_chain",
    )(rhs, maps)


def halves_kernel(mine_ref, pair_ref, high_ref, low_ref):
    b = mine_ref.shape[1]
    for k, ref in enumerate((mine_ref, pair_ref)):
        for i in range(ref.shape[0]):
            high_ref[i, k * b : (k + 1) * b], low_ref[i, k * b : (k + 1) * b] = split(ref[i])


def halves(mine, pair):
    leaves, b, _ = mine.shape
    block = pl.BlockSpec((STEP, b, b), lambda i: (i, 0, 0))
    out = pl.BlockSpec((STEP, 2 * b, b), lambda i: (i, 0, 0))
    return pl.pallas_call(
        halves_kernel,
        grid=(leaves // STEP,),
        in_specs=[block] * 2,
        out_specs=[out] * 2,
        out_shape=[jax.ShapeDtypeStruct((leaves, 2 * b, b), BF16)] * 2,
        name="halves",
    )(mine, pair)


def leaf_backward_kernel(place_ref, targets_ref, tops_ref, *refs):
    high_ref, low_ref, *block_refs, own_ref, inv_ref, out_ref, parts = refs
    core, y, _, row = (place_ref[k] for k in range(4))
    step = pl.program_id(0)
    n_cols = len(block_refs) + 2
    count, b, _ = block_refs[0].shape
    own = own_ref.shape[1]
    slab = b // n_cols
    leaf_rows = out_ref.shape[1] - own

    @pl.when(step == 0)
    def _():
        for t in range(parts.shape[0]):
            high, low = split(tops_ref[t])
            parts[t, :own] = high
            parts[t, own:] = low
        for c in range(n_cols):
            out_ref[c, leaf_rows:] = tops_ref[row]

    results = []
    for i in range(count):
        leaf = step * count + i
        both = jnp.concatenate(
            [
                parts[targets_ref[2 * ((y + k // 2) % (n_cols // 2)) + (core + k) % 2, leaf]]
                for k in range(n_cols)
            ],
            axis=1,
        )
        high, low = split(jnp.concatenate([ref[i] for ref in block_refs], axis=0))
        high = jnp.concatenate([high_ref[i], high], axis=0)
        low = jnp.concatenate([low_ref[i], low], axis=0)
        r = dot(both, high)
        left = own_ref[i] - ((r[:own] + r[own:]) + dot(both[:own], low))
        results.append(dot3(left, inv_ref[:, i].reshape(b, b)))
    turned = jnp.concatenate(results, axis=0).T
    for c in range(n_cols):
        out_ref[c, pl.ds(pl.multiple_of(step * slab, slab), slab)] = turned[
            c * slab : (c + 1) * slab
        ]


def leaf_backward(place, targets, tops, near, blocks, own, inv):
    n_cols = len(blocks) + 2
    leaves, b, _ = blocks[0].shape
    mine = own.shape[1]
    slab = b // n_cols
    step = b // mine
    out = (n_cols, leaves // step * slab + mine, b)
    return pl.pallas_call(
        leaf_backward_kernel,
        grid_spec=pltpu.PrefetchScalarGridSpec(
            num_scalar_prefetch=2,
            grid=(leaves // step,),
            in_specs=[whole(tops.shape)]
            + [pl.BlockSpec((step, 2 * b, b), lambda i, *_: (i, 0, 0))] * 2
            + [pl.BlockSpec((step, b, b), lambda i, *_: (i, 0, 0))] * len(blocks)
            + [
                pl.BlockSpec((step, mine, b), lambda i, *_: (i, 0, 0)),
                pl.BlockSpec((n_cols, step, slab, b), lambda i, *_: (0, i, 0, 0)),
            ],
            out_specs=whole(out),
            scratch_shapes=[pltpu.VMEM((tops.shape[0], 2 * mine, b), BF16)],
        ),
        out_shape=jax.ShapeDtypeStruct(out, F32),
        name="leaf_backward",
    )(place, targets, tops, *near, *blocks, own, inv)


def arrange_kernel(got_ref, leaf_ref, top_ref):
    n_cols, _, b = got_ref.shape
    leaves, slab, r = leaf_ref.shape
    own = r // n_cols
    step = b // own
    groups = leaves // step
    for h in range(2):
        for g in range(groups):
            for i in range(step):
                leaf_ref[g * step + i, :, h * b : (h + 1) * b] = jnp.concatenate(
                    [
                        got_ref[2 * q + h, g * slab : (g + 1) * slab, i * own : (i + 1) * own]
                        for q in range(step)
                    ],
                    axis=1,
                )
        top_ref[0, :, h * b : (h + 1) * b] = jnp.concatenate(
            [got_ref[2 * q + h, groups * slab :] for q in range(step)], axis=0
        ).T


def arrange(got, leaves, r):
    n_cols, _, b = got.shape
    return pl.pallas_call(
        arrange_kernel,
        out_shape=[
            jax.ShapeDtypeStruct((leaves, b // n_cols, r), F32),
            jax.ShapeDtypeStruct((1, b, r), F32),
        ],
        name="arrange",
    )(got)


def spread(x, axis):
    n = lax.axis_size(axis)
    return lax.all_to_all(jnp.broadcast_to(x, (n,) + x.shape), axis, 0, 0, tiled=True)


def from_core(x):
    return lax.ppermute(x, "core", [(0, 1), (1, 0)])


def from_y(x, step):
    n = lax.axis_size("y")
    return lax.ppermute(x, "y", [(i, (i - step) % n) for i in range(n)])


def on_device(known, pivot, leaf_blocks, leaf_target, top_rhs, top_inv, top_sub):
    leaves, b, r = known.shape
    n_y = lax.axis_size("y")
    n_cols = 2 * n_y
    tops = lax.axis_size(ROWS)
    y = lax.axis_index("y")
    core = lax.axis_index("core")
    row = lax.axis_index(ROWS)
    blocks = leaf_blocks[:, 0]
    slab = pivot.shape[1]
    own = r // n_cols

    packed, own_maps = prepare(leaf_target[:, 0], pivot, top_inv, top_sub, n_cols)
    inv = lax.all_to_all(packed, COLS, 0, 0, tiled=True)
    maps = lax.all_gather(own_maps, ROWS, axis=0, tiled=False)
    paired = from_core(blocks)
    far = [from_y(blocks, 1), None, from_y(blocks, 3)]
    targets = inv[:, leaves, :leaves, 0].astype(jnp.int32)

    part = y * lax.axis_size("layers") + lax.axis_index("layers")
    place = jnp.stack([core, y, part, row])
    rhs_t = lax.dynamic_slice_in_dim(top_rhs[0], core * (r // 2) + part * 8, 8, 1).T
    sums, own_forward = leaf_forward(place, targets, rhs_t, inv, blocks, paired, known, tops)
    near, sums = lax.optimization_barrier(((blocks, paired), sums))
    near = halves(*near)
    partial = lax.all_to_all(sums, ("y", "layers"), 0, 0, tiled=True)
    partial, near = lax.optimization_barrier((partial, near))
    partial = partial.sum(0)

    quarter = lax.all_to_all(partial, "rlo", 0, 0, tiled=True)
    quarter = quarter.reshape((lax.axis_size("rlo"), -1) + quarter.shape[1:]).sum(0)
    held, quarter = lax.optimization_barrier((blocks, quarter))
    far[1] = from_y(held, 2)
    quarter = spread(quarter, "rhi").sum(0)
    quarter, far[0], far[2] = lax.optimization_barrier((quarter, far[0], far[2]))
    all_blocks = []
    for block in far:
        all_blocks += [block, from_core(block)]
    rhs = spread(quarter, ("rlo", "layers"))
    rhs = rhs.reshape((lax.axis_size("rlo"), -1) + rhs.shape[1:])

    own_tops = top_chain(rhs, maps)
    turned = leaf_backward(place, targets, own_tops, near, all_blocks, own_forward, inv)
    got = lax.all_to_all(turned, COLS, 0, 0, tiled=True)
    return tuple(arrange(got, leaves, r))


def solution(mesh):
    rows = mesh.shape["rows"]
    low = 4
    fine = Mesh(
        mesh.devices.reshape(
            rows // low, low, mesh.shape["cols"] // 2, 2, mesh.shape["layers"]
        ),
        ROWS + COLS + ("layers",),
    )
    held = ROWS + ("layers",)
    in_specs = (
        P(held, None, None),
        P(held, COLS, None),
        P(held, COLS, None, None),
        P(held, COLS),
        P(ROWS, None, None),
        P(ROWS, None, None),
        P(ROWS, None, None),
    )
    out_specs = (P(held, COLS, None), P(ROWS, None, None))
    return jax.shard_map(
        on_device, mesh=fine, in_specs=in_specs, out_specs=out_specs, check_vma=False
    )
```

```python
import jax
import jax.numpy as jnp
from jax import lax
from jax.experimental import pallas as pl
from jax.experimental.pallas import tpu as pltpu
from jax.sharding import Mesh, PartitionSpec as P

F32 = jnp.float32
BF16 = jnp.bfloat16
ROWS = ("rhi", "rlo")
COLS = ("y", "core")
STEP = 6


def dot(a, b, cb=0):
    return lax.dot_general(a, b, (((1,), (cb,)), ((), ())), preferred_element_type=F32)


def split(x):
    high = x.astype(BF16)
    low = (x - high.astype(F32)).astype(BF16)
    return high, low


def dot3(a, b, cb=0):
    ah, al = split(a)
    bh, bl = split(b)
    both = dot(
        jnp.concatenate([ah, al], axis=1), jnp.concatenate([bh, bh], axis=cb), cb
    )
    return both + dot(ah, bl, cb)


def row_dot(x, matrix, cb=0):
    n = x.shape[0]
    m = matrix.shape[1 - cb]
    rows = jnp.concatenate(split(x), axis=0)
    r = dot(rows, jnp.concatenate(split(matrix), axis=1 - cb), cb)
    return (r[:n, :m] + (r[n:, :m] + r[:n, m:])) + r[n:, m:]


def whole(shape):
    return pl.BlockSpec(shape, lambda *_: (0,) * len(shape))


def prepare_kernel(targets_ref, pivot_ref, inv_ref, sub_ref, out_ref, maps_ref):
    leaves, slab, b = pivot_ref.shape
    line = lax.broadcasted_iota(jnp.int32, (slab, b), 0)
    named = jnp.zeros((slab, b), F32)
    for i in range(leaves):
        named = jnp.where(line == i, targets_ref[i].astype(F32), named)
    for c in range(out_ref.shape[0]):
        out_ref[c, :leaves] = pivot_ref[...]
        out_ref[c, leaves] = named
    maps_ref[0] = inv_ref[0]
    maps_ref[1] = -lax.dot_general(
        inv_ref[0],
        sub_ref[0],
        (((1,), (0,)), ((), ())),
        precision=lax.Precision.HIGHEST,
        preferred_element_type=F32,
    )


def prepare(targets, pivot, inv, sub, n_cols):
    leaves, slab, b = pivot.shape
    vmem = pl.BlockSpec(memory_space=pltpu.VMEM)
    return pl.pallas_call(
        prepare_kernel,
        in_specs=[pl.BlockSpec(memory_space=pltpu.SMEM), vmem, vmem, vmem],
        out_specs=[vmem, vmem],
        out_shape=[
            jax.ShapeDtypeStruct((n_cols, leaves + 1, slab, b), F32),
            jax.ShapeDtypeStruct((2,) + inv.shape[1:], F32),
        ],
        name="prepare",
    )(targets, pivot, inv, sub)


def leaf_forward_kernel(place_ref, targets_ref, rhs_ref, inv_ref, mine_ref, pair_ref, known_ref, sums_ref, own_ref, stage):
    core, y, part, row = (place_ref[k] for k in range(4))
    step = pl.program_id(0)
    count, b = mine_ref.shape[:2]
    own = own_ref.shape[1]
    n_y = known_ref.shape[2] // own
    layers = sums_ref.shape[0] // n_y

    @pl.when(step == 0)
    def _():
        sums_ref[...] = jnp.zeros_like(sums_ref)
        sums_ref[part % layers * n_y + part // layers, row] = rhs_ref[...]

    for i in range(count):
        inv = inv_ref[:, i].reshape(b, b)
        forward = dot3(known_ref[i].T, inv, 1)
        update = dot3(forward, jnp.concatenate([mine_ref[i], pair_ref[i]], axis=0), 1)
        for k in range(2):
            t = targets_ref[2 * y + (core if k == 0 else 1 - core), step * count + i]
            for q in range(sums_ref.shape[0]):
                sums_ref[q % layers * n_y + q // layers, t] -= update[8 * q : 8 * q + 8, k * b : (k + 1) * b]
        stage[i] = forward
        own_ref[i] = stage[i, pl.ds(pl.multiple_of(y * own, own), own), :]


def leaf_forward(place, targets, rhs, inv, mine, pair, known, tops):
    leaves, b, r = known.shape
    n_cols, _, slab, _ = inv.shape
    half = r // 2
    own = r // n_cols
    block = pl.BlockSpec((STEP, b, b), lambda i, *_: (i, 0, 0))
    return pl.pallas_call(
        leaf_forward_kernel,
        grid_spec=pltpu.PrefetchScalarGridSpec(
            num_scalar_prefetch=2,
            grid=(leaves // STEP,),
            in_specs=[
                whole(rhs.shape),
                pl.BlockSpec((n_cols, STEP, slab, b), lambda i, *_: (0, i, 0, 0)),
                block,
                block,
                pl.BlockSpec((STEP, b, half), lambda i, place, _: (i, 0, place[0])),
            ],
            out_specs=[
                whole((half // 8, tops, 8, b)),
                pl.BlockSpec((STEP, own, b), lambda i, *_: (i, 0, 0)),
            ],
            scratch_shapes=[pltpu.VMEM((STEP, half, b), F32)],
        ),
        out_shape=[
            jax.ShapeDtypeStruct((half // 8, tops, 8, b), F32),
            jax.ShapeDtypeStruct((leaves, own, b), F32),
        ],
        name="leaf_forward",
    )(place, targets, rhs, inv, mine, pair, known)


def top_chain_kernel(rhs_ref, maps_ref, out_ref):
    low, layers, high, n, b = rhs_ref.shape
    tops = low * high

    def rhs(t):
        return rhs_ref[t // high, :, t % high].reshape(layers * n, b)

    def maps(t, kind):
        return maps_ref[t, kind]

    pairs = [None] + [dot3(maps(t + 1, 1), maps(t, 1)) for t in range(2, tops, 2)]
    local = [row_dot(rhs(t), maps(t, 0), 1) for t in range(tops)]
    both = [local[t + 1] + row_dot(local[t], maps(t + 1, 1), 1) for t in range(0, tops, 2)]
    odd = [both[0]]
    for k in range(1, tops // 2):
        odd.append(both[k] + row_dot(odd[-1], pairs[k], 1))
    solved = []
    for k in range(tops // 2):
        t = 2 * k
        solved.append(local[t] + row_dot(odd[k - 1], maps(t, 1), 1) if k else local[0])
        solved.append(odd[k])
    rest = [None] * tops
    rest[tops - 1] = solved[tops - 1]
    for k in range(tops // 2 - 1, 0, -1):
        ahead = solved[2 * k - 1] + row_dot(solved[2 * k], maps(2 * k, 1))
        rest[2 * k - 1] = ahead + row_dot(rest[2 * k + 1], pairs[k])
    for t in range(tops - 2, -1, -2):
        rest[t] = solved[t] + row_dot(rest[t + 1], maps(t + 1, 1))
    for t in range(tops):
        out_ref[t] = row_dot(rest[t], maps(t, 0))


def top_chain(rhs, maps):
    low, layers, high, n, b = rhs.shape
    return pl.pallas_call(
        top_chain_kernel,
        out_shape=jax.ShapeDtypeStruct((low * high, layers * n, b), F32),
        name="top_chain",
    )(rhs, maps)


def leaf_backward_kernel(place_ref, targets_ref, tops_ref, *refs):
    *block_refs, own_ref, inv_ref, out_ref, parts = refs
    core, y, _, row = (place_ref[k] for k in range(4))
    step = pl.program_id(0)
    n_cols = len(block_refs)
    count, b, _ = block_refs[0].shape
    own = own_ref.shape[1]
    slab = b // n_cols
    leaf_rows = out_ref.shape[1] - own

    @pl.when(step == 0)
    def _():
        for t in range(parts.shape[0]):
            high, low = split(tops_ref[t])
            parts[t, :own] = high
            parts[t, own:] = low
        for c in range(n_cols):
            out_ref[c, leaf_rows:] = tops_ref[row]

    results = []
    for i in range(count):
        leaf = step * count + i
        both = jnp.concatenate(
            [
                parts[targets_ref[2 * ((y + k // 2) % (n_cols // 2)) + (core + k) % 2, leaf]]
                for k in range(n_cols)
            ],
            axis=1,
        )
        high, low = split(jnp.concatenate([ref[i] for ref in block_refs], axis=0))
        r = dot(both, high)
        left = own_ref[i] - ((r[:own] + r[own:]) + dot(both[:own], low))
        results.append(dot3(left, inv_ref[:, i].reshape(b, b)))
    turned = jnp.concatenate(results, axis=0).T
    for c in range(n_cols):
        out_ref[c, pl.ds(pl.multiple_of(step * slab, slab), slab)] = turned[
            c * slab : (c + 1) * slab
        ]


def leaf_backward(place, targets, tops, blocks, own, inv):
    n_cols = len(blocks)
    leaves, b, _ = blocks[0].shape
    mine = own.shape[1]
    slab = b // n_cols
    step = b // mine
    out = (n_cols, leaves // step * slab + mine, b)
    return pl.pallas_call(
        leaf_backward_kernel,
        grid_spec=pltpu.PrefetchScalarGridSpec(
            num_scalar_prefetch=2,
            grid=(leaves // step,),
            in_specs=[whole(tops.shape)]
            + [pl.BlockSpec((step, b, b), lambda i, *_: (i, 0, 0))] * n_cols
            + [
                pl.BlockSpec((step, mine, b), lambda i, *_: (i, 0, 0)),
                pl.BlockSpec((n_cols, step, slab, b), lambda i, *_: (0, i, 0, 0)),
            ],
            out_specs=whole(out),
            scratch_shapes=[pltpu.VMEM((tops.shape[0], 2 * mine, b), BF16)],
        ),
        out_shape=jax.ShapeDtypeStruct(out, F32),
        name="leaf_backward",
    )(place, targets, tops, *blocks, own, inv)


def arrange_kernel(got_ref, leaf_ref, top_ref):
    n_cols, _, b = got_ref.shape
    leaves, slab, r = leaf_ref.shape
    own = r // n_cols
    step = b // own
    groups = leaves // step
    for h in range(2):
        for g in range(groups):
            for i in range(step):
                leaf_ref[g * step + i, :, h * b : (h + 1) * b] = jnp.concatenate(
                    [
                        got_ref[2 * q + h, g * slab : (g + 1) * slab, i * own : (i + 1) * own]
                        for q in range(step)
                    ],
                    axis=1,
                )
        top_ref[0, :, h * b : (h + 1) * b] = jnp.concatenate(
            [got_ref[2 * q + h, groups * slab :] for q in range(step)], axis=0
        ).T


def arrange(got, leaves, r):
    n_cols, _, b = got.shape
    return pl.pallas_call(
        arrange_kernel,
        out_shape=[
            jax.ShapeDtypeStruct((leaves, b // n_cols, r), F32),
            jax.ShapeDtypeStruct((1, b, r), F32),
        ],
        name="arrange",
    )(got)


def spread(x, axis):
    n = lax.axis_size(axis)
    return lax.all_to_all(jnp.broadcast_to(x, (n,) + x.shape), axis, 0, 0, tiled=True)


def from_core(x):
    return lax.ppermute(x, "core", [(0, 1), (1, 0)])


def from_y(x, step):
    n = lax.axis_size("y")
    return lax.ppermute(x, "y", [(i, (i - step) % n) for i in range(n)])


def on_device(known, pivot, leaf_blocks, leaf_target, top_rhs, top_inv, top_sub):
    leaves, b, r = known.shape
    n_y = lax.axis_size("y")
    n_cols = 2 * n_y
    tops = lax.axis_size(ROWS)
    y = lax.axis_index("y")
    core = lax.axis_index("core")
    row = lax.axis_index(ROWS)
    blocks = leaf_blocks[:, 0]
    slab = pivot.shape[1]
    own = r // n_cols

    packed, own_maps = prepare(leaf_target[:, 0], pivot, top_inv, top_sub, n_cols)
    inv = lax.all_to_all(packed, COLS, 0, 0, tiled=True)
    maps = lax.all_gather(own_maps, ROWS, axis=0, tiled=False)
    paired = from_core(blocks)
    far = [from_y(blocks, 1), None, from_y(blocks, 3)]
    targets = inv[:, leaves, :leaves, 0].astype(jnp.int32)

    part = y * lax.axis_size("layers") + lax.axis_index("layers")
    place = jnp.stack([core, y, part, row])
    rhs_t = lax.dynamic_slice_in_dim(top_rhs[0], core * (r // 2) + part * 8, 8, 1).T
    sums, own_forward = leaf_forward(place, targets, rhs_t, inv, blocks, paired, known, tops)
    partial = lax.all_to_all(sums, ("layers", "y"), 0, 0, tiled=True).sum(0)

    quarter = lax.all_to_all(partial, "rlo", 0, 0, tiled=True)
    quarter = quarter.reshape((lax.axis_size("rlo"), -1) + quarter.shape[1:]).sum(0)
    held, quarter = lax.optimization_barrier((blocks, quarter))
    far[1] = from_y(held, 2)
    quarter = spread(quarter, "rhi").sum(0)
    quarter, far[0], far[2] = lax.optimization_barrier((quarter, far[0], far[2]))
    all_blocks = [blocks, paired]
    for block in far:
        all_blocks += [block, from_core(block)]
    rhs = spread(quarter, ("rlo", "layers"))
    rhs = rhs.reshape((lax.axis_size("rlo"), -1) + rhs.shape[1:])

    own_tops = top_chain(rhs, maps)
    turned = leaf_backward(place, targets, own_tops, all_blocks, own_forward, inv)
    got = lax.all_to_all(turned, COLS, 0, 0, tiled=True)
    return tuple(arrange(got, leaves, r))


def solution(mesh):
    rows = mesh.shape["rows"]
    low = 4
    fine = Mesh(
        mesh.devices.reshape(
            rows // low, low, mesh.shape["cols"] // 2, 2, mesh.shape["layers"]
        ),
        ROWS + COLS + ("layers",),
    )
    held = ROWS + ("layers",)
    in_specs = (
        P(held, None, None),
        P(held, COLS, None),
        P(held, COLS, None, None),
        P(held, COLS),
        P(ROWS, None, None),
        P(ROWS, None, None),
        P(ROWS, None, None),
    )
    out_specs = (P(held, COLS, None), P(ROWS, None, None))
    return jax.shard_map(
        on_device, mesh=fine, in_specs=in_specs, out_specs=out_specs, check_vma=False
    )
```
